32 devices in a mesh: lat: 4 (over z), fld: 4 (over y, x), rep: 2 (over core).
Axes of the slice: x: 2, y: 2, z: 4, core: 2. Of those that a mesh axis runs over, the one named last changes fastest.
Arguments:
- field: float32 [12, 1280, 2560], P('fld', ('lat', 'rep')), may hold values from -6 to 6
- wind_zonal: float32 [12, 1280, 2560], P('fld', ('lat', 'rep')), may hold values from -4 to 4
- wind_merid: float32 [12, 1280, 2560], P('fld', ('lat', 'rep')), may hold values from -4 to 4
- band: int32 [12, 2], replicated, may hold values from 0 to 1280, as said below
- waves: int32 [16, 80], replicated, may hold values from -1 to 1279, as said below
- legendre: bfloat16 [16, 1280, 51328], P(('lat', 'fld')), may hold values from -0.15625 to 0.15625
Outputs:
- spectrum: float32 [16, 12, 2, 51328], P(('lat', 'fld'), 'rep')
The draws below stay inside these ranges and needn't reach their ends.
Inputs may be any that keep to these rules, and one draw needn't show every extreme that they name: band[f, 0] is below 320 and band[f, 1] is above 960, for every field-level. `waves`: every wavenumber 0 to 1279 stands in exactly one slot of one group; -1 marks an empty slot. Wavenumber m takes 1280 - m columns, and the wavenumbers of one group take at most 51240 columns together; some group takes exactly 51240.
All inputs are finite; a program needn't handle non-finite values.
Results may differ from the reference program's by a relative error of at most 0.0056.
Values may be sent and summed in bfloat16 or wider, within the bound.
A program may use at most 256 MiB of HBM per device.

```python
import math
import jax
import jax.numpy as jnp
from jax import lax

NLAT = 1280
NLON = 2560
M = 1280
F = 12
GROUPS = 16
ROUNDS = 40
REST = 0
SLOTS = 80
COLS = 51328


def draw_band(key, part):
    keys = jax.random.split(jax.random.fold_in(key, 11), 4)
    quarter = NLAT // 4
    lower_rows = jax.random.randint(keys[0], (F,), 0, quarter)
    upper_rows = NLAT - jax.random.randint(keys[1], (F,), 0, quarter)
    lower_rows = lower_rows.at[jax.random.randint(keys[2], (), 0, F)].set(0)
    upper_rows = upper_rows.at[jax.random.randint(keys[3], (), 0, F)].set(NLAT)
    return jnp.stack([lower_rows, upper_rows], axis=1).astype(jnp.int32)


def draw_waves(key, part):
    base_key = jax.random.fold_in(key, 23)
    assignment = -jnp.ones((GROUPS, SLOTS), jnp.int32)
    positions = jnp.arange(GROUPS, dtype=jnp.int32)
    for round_index in range(ROUNDS):
        ordering = jax.random.permutation(jax.random.fold_in(base_key, round_index), GROUPS)
        first_waves = 2 * round_index * GROUPS + positions
        second_waves = (2 * round_index + 2) * GROUPS - 1 - positions
        assignment = assignment.at[ordering, 2 * round_index].set(first_waves)
        assignment = assignment.at[ordering, 2 * round_index + 1].set(second_waves)
    if REST > 0:
        ordering = jax.random.permutation(jax.random.fold_in(base_key, ROUNDS + 7), GROUPS)
        rest_waves = jnp.where(positions < REST, 2 * ROUNDS * GROUPS + positions, -1).astype(jnp.int32)
        assignment = assignment.at[ordering, 2 * ROUNDS].set(rest_waves)
    slot_scores = jax.random.randint(jax.random.fold_in(base_key, 5003), (GROUPS, SLOTS), 0, 1 << 20)
    slot_scores = slot_scores * SLOTS + jnp.arange(SLOTS, dtype=jnp.int32)[None, :]
    shuffle = jnp.argsort(slot_scores, axis=1)
    return jnp.take_along_axis(assignment, shuffle, axis=1).astype(jnp.int32)


def block_levels(key, shape, cuts, low, largest):
    def one(position, blocks):
        heights = jax.random.uniform(jax.random.fold_in(jax.random.fold_in(key, 6), position), (blocks,), jnp.float32, low / len(cuts), largest / len(cuts))
        return jnp.repeat(jnp.exp(heights), shape[position] // blocks).reshape((-1,) + (1,) * (len(shape) - position - 1))

    loudness = one(*cuts[0])
    for cut in cuts[1:]:
        loudness = loudness * one(*cut)
    return loudness


def scatter_about(stream_key, dims, scale, limit, shards=(), held_as=jnp.bfloat16):
    drawn = jax.random.normal(stream_key, dims, jnp.float32) * scale
    if len(shards) > 0:
        drawn = block_levels(stream_key, dims, shards, -0.22, 0.18) * drawn
    return jnp.clip(drawn, min=-limit, max=limit).astype(held_as)


def setup_inputs(seed: int = 0) -> dict:
    seeds = jax.random.split(jax.random.key(seed), 7)
    field = scatter_about(seeds[0], (F, NLAT, NLON), 1.0, 6.0, ((0, 4), (1, 8)), jnp.float32)
    wind_zonal = scatter_about(seeds[1], (F, NLAT, NLON), 1.0, 4.0, ((0, 4), (1, 8)), jnp.float32)
    wind_merid = scatter_about(seeds[2], (F, NLAT, NLON), 1.0, 4.0, ((0, 4), (1, 8)), jnp.float32)
    band = draw_band(jax.random.fold_in(seeds[6], 71), 0)
    waves = draw_waves(jax.random.fold_in(seeds[6], 71), 0)
    legendre = scatter_about(seeds[5], (GROUPS, NLAT, COLS), NLAT ** -0.5, 0.15625, ((0, 16),))
    return {"field": field, "wind_zonal": wind_zonal, "wind_merid": wind_merid, "band": band, "waves": waves, "legendre": legendre}


def dft_matrix(lon_count, wave_count):
    lon_ids = lax.broadcasted_iota(jnp.int32, (lon_count, wave_count), 0)
    wave_ids = lax.broadcasted_iota(jnp.int32, (lon_count, wave_count), 1)
    angles = (lon_ids * wave_ids % lon_count).astype(jnp.float32) * (2.0 * math.pi / lon_count)
    scaling = 1.0 / math.sqrt(lon_count)
    return jnp.concatenate([jnp.cos(angles) * scaling, -jnp.sin(angles) * scaling], axis=1).astype(jnp.bfloat16)

def tendency(centre, above_row, below_row, zonal_wind, merid_wind):
    eastward = jnp.roll(centre, -1, axis=-1)
    westward = jnp.roll(centre, 1, axis=-1)
    return -(zonal_wind + centre) * (eastward - westward) * 0.5 - merid_wind * (above_row - below_row) * 0.5

def reference(field, wind_zonal, wind_merid, band, waves, legendre):
    matrix = dft_matrix(NLON, M)
    row_ids = jnp.arange(NLAT).astype(jnp.int32)[:, None]

    def one_field(inputs):
        values, zonal_wind, merid_wind, bounds = inputs
        in_band = ((row_ids >= bounds[0]) & (row_ids < bounds[1])).astype(jnp.float32)
        padded = jnp.pad(values, ((1, 1), (0, 0)))
        first_section = values + in_band * tendency(values, padded[2:], padded[:-2], zonal_wind, merid_wind)
        padded_section = jnp.pad(first_section, ((1, 1), (0, 0)))
        advected = 0.5 * (values + first_section + in_band * tendency(first_section, padded_section[2:], padded_section[:-2], zonal_wind, merid_wind))
        grid_low = advected.astype(jnp.bfloat16)
        return jnp.dot(grid_low, matrix, preferred_element_type=jnp.float32).astype(jnp.bfloat16)
    spectra = lax.map(one_field, (field, wind_zonal, wind_merid, band))
    spectra = spectra.reshape(F, NLAT, 2, M)
    col_ids = jnp.arange(COLS).astype(jnp.int32)

    def one_group(inputs):
        own_waves, columns = inputs
        own_filled = own_waves >= 0
        wave_index = jnp.where(own_filled, own_waves, 0).astype(jnp.int32)
        counts = jnp.where(own_filled, M - own_waves, 0).astype(jnp.int32)
        offsets = (jnp.cumsum(counts) - counts).astype(jnp.int32)
        segments = ((col_ids[None, :] >= offsets[:, None]) & (col_ids[None, :] < (offsets + counts)[:, None])).astype(jnp.float32)
        picked = jnp.take(spectra, wave_index, axis=3).astype(jnp.float32)
        products = jnp.einsum('flcs,lk->sfck', picked, columns.astype(jnp.float32))
        return jnp.einsum('sfck,sk->fck', products, segments)
    return lax.map(one_group, (waves, legendre))
```

```python
import functools
import math

import jax
import jax.numpy as jnp
import ml_dtypes
import numpy as np
from jax import lax
from jax.experimental import pallas as pl
from jax.experimental.pallas import tpu as pltpu
from jax.sharding import PartitionSpec as P

M = 1280
LANES = 128
SUB = 16
TILE = 512
WINDOW = 8
RING = 10
PAD = 16
MESH = pl.DeviceIdType.MESH


def with_halo(value, sides, width):
    for axis, dim in sides:
        peers, length = (lax.axis_size(axis), value.shape[dim])
        up = [(i, (i + 1) % peers) for i in range(peers - 1)]
        down = [(j, i) for i, j in up]
        last = lax.slice_in_dim(value, length - width, length, axis=dim)
        first = lax.slice_in_dim(value, 0, width, axis=dim)
        before = lax.ppermute(last, axis, up)
        after = lax.ppermute(first, axis, down)
        value = jnp.concatenate([before, value, after], axis=dim)
    return value


def dft_matrix(lon_count, wave_count):
    lon_ids = lax.broadcasted_iota(jnp.int32, (lon_count, wave_count), 0)
    wave_ids = lax.broadcasted_iota(jnp.int32, (lon_count, wave_count), 1)
    angles = (lon_ids * wave_ids % lon_count).astype(jnp.float32) * (2.0 * math.pi / lon_count)
    scaling = 1.0 / math.sqrt(lon_count)
    return jnp.concatenate([jnp.cos(angles) * scaling, -jnp.sin(angles) * scaling], axis=1).astype(
        jnp.bfloat16
    )


def tendency(centre, above_row, below_row, zonal_wind, merid_wind):
    eastward = jnp.roll(centre, -1, axis=-1)
    westward = jnp.roll(centre, 1, axis=-1)
    return (
        -(zonal_wind + centre) * (eastward - westward) * 0.5
        - merid_wind * (above_row - below_row) * 0.5
    )


def band_mask(bounds, first_row, row_total):
    row_ids = first_row + lax.broadcasted_iota(jnp.int32, (1, row_total, 1), 1)
    lower_edge = bounds[:, 0][:, None, None]
    upper_edge = bounds[:, 1][:, None, None]
    return ((row_ids >= lower_edge) & (row_ids < upper_edge)).astype(jnp.float32)


def folded_matrix(lon_count):
    half = lon_count // 2
    waves = np.arange(M).reshape(M // 2, 2).T.reshape(2, 1, M // 2, 1)
    turns = (waves * np.arange(half)) % lon_count
    angles = turns * (2.0 * math.pi / lon_count)
    both = np.concatenate([np.cos(angles), -np.sin(angles)], axis=1) / math.sqrt(lon_count)
    return both.reshape(2 * M, half).astype(ml_dtypes.bfloat16)


def schedule(slots, cols):
    chunks = slots // SUB
    phases = [0]
    for tile in range(cols // TILE):
        share = min(1.0, (tile + 1) * TILE / cols)
        needed = share * slots + 3.5 * math.sqrt(slots * share * (1.0 - share) / 3.0) + 1.0
        phase = min(chunks - 1, math.ceil(needed / SUB) - 1)
        phases.append(max(phases[-1], phase))
    return phases[1:] + [chunks - 1]


def flipped(value, bits, size):
    result, bit = 0, 1
    while bit < size:
        digit = (value // bit) % 2
        result = result + bit * ((1 - digit) if bits & bit else digit)
        bit *= 2
    return result


def fused_kernel(
    dims,
    band,
    base,
    starts,
    order,
    field,
    zonal,
    merid,
    matrix_source,
    legendre,
    out,
    kept,
    x,
    section,
    wind_zonal,
    wind_merid,
    edge,
    halo_out,
    halo_in,
    folded,
    matrix,
    natural,
    pick,
    outgoing,
    received,
    stage,
    ordered,
    ring_main,
    ring_rest,
    tail_main,
    tail_rest,
    total,
    edge_sem,
    field_sem,
    matrix_sem,
    halo_send,
    halo_recv,
    send_sem,
    recv_sem,
    own_sem,
    ring_sem,
    tail_sem,
    kept_sem,
    out_sem,
):
    lat_size, fld_size, rep_size = dims
    lat, fld, rep = lax.axis_index("lat"), lax.axis_index("fld"), lax.axis_index("rep")
    levels, rows, length = field.shape
    parts = length // LANES
    half = parts // 2
    groups = lat_size * fld_size
    chunks, origins = received.shape[0], received.shape[1]
    bands = lat_size * rep_size
    rest = rows - LANES
    width = folded.shape[1]
    position = lat * rep_size + rep
    peers = bands
    waves_half = M // 2
    cols = legendre.shape[2]
    tiles = cols // TILE
    tail = cols - tiles * TILE
    start = position * rows

    edge_copies = []
    for side, first in enumerate((0, rows - 8)):
        for array, source in enumerate((field, zonal, merid)):
            edge_copies.append(
                pltpu.make_async_copy(
                    source.at[:, first : first + 8, :], edge.at[side, array], edge_sem.at[side, array]
                )
            )
    for copy in edge_copies:
        copy.start()

    def column_copy(level, part):
        return pltpu.make_async_copy(
            field.at[level, :, pl.ds(pl.multiple_of(part * LANES, LANES), LANES)],
            x.at[level, part, PAD : PAD + rows, :],
            field_sem.at[level, part],
        )

    def wind_copies(level):
        return (
            pltpu.make_async_copy(
                zonal.at[level], wind_zonal.at[level, 8 : 8 + rows, :], field_sem.at[level, parts]
            ),
            pltpu.make_async_copy(
                merid.at[level], wind_merid.at[level, 8 : 8 + rows, :], field_sem.at[level, parts + 1]
            ),
        )

    @pl.loop(0, levels)
    def _(level):
        @pl.loop(0, parts)
        def _(part):
            column_copy(level, part).start()

        for copy in wind_copies(level):
            copy.start()

    matrix_copy = pltpu.make_async_copy(matrix_source, matrix, matrix_sem)
    matrix_copy.start()

    above = lax.rem(position + peers - 1, peers)
    below = lax.rem(position + 1, peers)

    def halo_copy(side):
        target = (above, below)[side]
        return pltpu.make_async_remote_copy(
            src_ref=halo_out.at[side],
            dst_ref=halo_in.at[1 - side],
            send_sem=halo_send.at[side],
            recv_sem=halo_recv.at[1 - side],
            device_id=(target // rep_size, fld, target % rep_size),
            device_id_type=MESH,
        )

    exists = (position > 0, position < peers - 1)
    for copy in edge_copies:
        copy.wait()
    for part in range(parts):
        lanes = slice(part * LANES, (part + 1) * LANES)
        for level in range(levels):
            for side, (pair, single) in enumerate((((0, 2), (0, 1)), ((6, 8), (7, 8)))):
                halo_out[side, part, 2 * level : 2 * level + 2, :] = edge[
                    side, 0, level, pair[0] : pair[1], lanes
                ]
                for array in (1, 2):
                    row = (array + 1) * levels + level
                    halo_out[side, part, row : row + 1, :] = edge[
                        side, array, level, single[0] : single[1], lanes
                    ]
    for side in range(2):

        @pl.when(exists[side])
        def _():
            halo_copy(side).start()

        @pl.when(jnp.logical_not(exists[side]))
        def _():
            halo_in[side] = jnp.zeros(halo_in.shape[1:], jnp.float32)

    stage[...] = jnp.zeros(stage.shape, jnp.float32)
    filled = levels * rows
    folded[:, filled:width, :] = jnp.zeros((2, width - filled, folded.shape[2]), jnp.bfloat16)

    for side in range(2):

        @pl.when(exists[side])
        def _():
            halo_copy(1 - side).wait_recv()

    for part in range(parts):
        lanes = slice(part * LANES, (part + 1) * LANES)
        for level in range(levels):
            pair = slice(2 * level, 2 * level + 2)
            x[level, part, PAD - 2 : PAD, :] = halo_in[0, part, pair, :]
            x[level, part, PAD + rows : PAD + rows + 2, :] = halo_in[1, part, pair, :]
            for array, wind in ((1, wind_zonal), (2, wind_merid)):
                row = (array + 1) * levels + level
                wind[level, 7:8, lanes] = halo_in[0, part, row : row + 1, :]
                wind[level, 8 + rows : 9 + rows, lanes] = halo_in[1, part, row : row + 1, :]

    def slopes(centre_of, next_of, previous_of, zonal_of, merid_of, scale, last_lane, first_lane):
        centres, easts, wests = {}, {}, {}

        def turn(part):
            if part not in centres:
                centres[part] = centre_of(part)
                easts[part] = pltpu.roll(centres[part], LANES - 1, axis=1)
                wests[part] = pltpu.roll(centres[part], 1, axis=1)

        def slope(part):
            after, before = (part + 1) % parts, (part - 1) % parts
            for needed in (part, after, before):
                turn(needed)
            east = jnp.where(last_lane, easts[after], easts[part])
            west = jnp.where(first_lane, wests[before], wests[part])
            centre = centres[part]
            return centre, scale * (
                (zonal_of(part) + centre) * (west - east)
                + merid_of(part) * (previous_of(part) - next_of(part))
            )

        return slope

    def scale_of(level, first_row, count):
        lower, upper = band[0, fld * levels + level], band[1, fld * levels + level]
        ids = start + first_row + lax.broadcasted_iota(jnp.int32, (count, LANES), 0)
        return jnp.where((ids >= lower) & (ids < upper), 0.5, 0.0)

    def edges_of(count):
        lane = lax.broadcasted_iota(jnp.int32, (count, LANES), 1)
        return lane == LANES - 1, lane == 0

    @pl.loop(0, levels)
    def _(level):
        @pl.loop(0, parts)
        def _(part):
            column_copy(level, part).wait()

        for copy in wind_copies(level):
            copy.wait()

        @pl.loop(0, rows // 8 + 2)
        def _(block):
            first = pl.multiple_of(block * 8, 8)
            at = pl.multiple_of(first + PAD - 8, 8)
            slope = slopes(
                lambda part: x[level, part, pl.ds(at, 8), :],
                lambda part: x[level, part, pl.ds(at + 1, 8), :],
                lambda part: x[level, part, pl.ds(at - 1, 8), :],
                lambda part: wind_zonal[level, pl.ds(first, 8), part * LANES : (part + 1) * LANES],
                lambda part: wind_merid[level, pl.ds(first, 8), part * LANES : (part + 1) * LANES],
                scale_of(level, first - 8, 8),
                *edges_of(8),
            )
            for part in range(parts):
                centre, change = slope(part)
                section[part, pl.ds(at, 8), :] = centre + change

        @pl.loop(0, rows // SUB)
        def _(block):
            first = pl.multiple_of(block * SUB, SUB)
            at = pl.multiple_of(first + PAD, SUB)
            wind_at = pl.multiple_of(first + 8, 8)
            slope = slopes(
                lambda part: section[part, pl.ds(at, SUB), :],
                lambda part: section[part, pl.ds(at + 1, SUB), :],
                lambda part: section[part, pl.ds(at - 1, SUB), :],
                lambda part: wind_zonal[level, pl.ds(wind_at, SUB), part * LANES : (part + 1) * LANES],
                lambda part: wind_merid[level, pl.ds(wind_at, SUB), part * LANES : (part + 1) * LANES],
                scale_of(level, first, SUB),
                *edges_of(SUB),
            )

            def advected(part):
                centre, change = slope(part)
                return 0.5 * (x[level, part, pl.ds(at, SUB), :] + centre + change)

            late = first // LANES
            goes = (1 - late) * (level * LANES + first) + late * (
                levels * LANES + level * rest + first - LANES
            )
            goes = pl.ds(pl.multiple_of(goes, SUB), SUB)
            for part in range(half):
                near, far = advected(part), advected(part + half)
                lanes = slice(part * LANES, (part + 1) * LANES)
                folded[0, goes, lanes] = (near + far).astype(jnp.bfloat16)
                folded[1, goes, lanes] = (near - far).astype(jnp.bfloat16)

    def ring_copies(tile, slot):
        columns = pl.ds(pl.multiple_of(tile * TILE, TILE), TILE)
        return (
            pltpu.make_async_copy(
                legendre.at[:, 0:LANES, columns], ring_main.at[slot], ring_sem.at[slot, 0]
            ),
            pltpu.make_async_copy(
                legendre.at[:, LANES:rows, columns], ring_rest.at[slot], ring_sem.at[slot, 1]
            ),
        )

    for tile in range(min(RING, tiles)):
        for copy in ring_copies(tile, tile):
            copy.start()
    tail_columns = slice(tiles * TILE, cols)
    tail_copies = (
        pltpu.make_async_copy(legendre.at[:, 0:LANES, tail_columns], tail_main, tail_sem.at[0]),
        pltpu.make_async_copy(legendre.at[:, LANES:rows, tail_columns], tail_rest, tail_sem.at[1]),
    )
    for copy in tail_copies:
        copy.start()

    matrix_copy.wait()
    block_rows = waves_half // 2

    @pl.loop(0, 8)
    def _(block):
        parity, side, piece = block // 4, (block // 2) % 2, block % 2
        here = pl.ds(pl.multiple_of(block * block_rows, SUB), block_rows)
        there = pl.ds(pl.multiple_of(parity * waves_half + piece * block_rows, SUB), block_rows)
        natural[side, there, :] = lax.dot_general(
            matrix[here, :], folded[parity], (((1,), (1,)), ((), ())), preferred_element_type=jnp.float32
        ).astype(jnp.bfloat16)

    half_flds = fld_size // rep_size
    to_rep = fld // half_flds
    place = ((fld % half_flds) * lat_size + lat) * rep_size + rep
    own = lat * fld_size + fld
    stays = to_rep == rep
    hops = [(i, j) for i in range(lat_size - 1, -1, -1) for j in range(fld_size - 1, -1, -1)]

    def sending(chunk, index):
        far_lat = flipped(lat, hops[index][0], lat_size)
        far_fld = flipped(fld, hops[index][1], fld_size)
        return pltpu.make_async_remote_copy(
            src_ref=outgoing.at[chunk, far_lat * fld_size + far_fld],
            dst_ref=received.at[chunk, place],
            send_sem=send_sem.at[chunk, index],
            recv_sem=recv_sem.at[chunk, place],
            device_id=(far_lat, far_fld, to_rep),
            device_id_type=MESH,
        )

    def keeping(chunk):
        return pltpu.make_async_copy(
            outgoing.at[chunk, own], received.at[chunk, place], own_sem.at[chunk]
        )

    @pl.loop(0, chunks)
    def _(chunk):
        numbers = order[pl.ds(pl.multiple_of(chunk * SUB, SUB), SUB), :]
        lane = lax.broadcasted_iota(jnp.int32, (SUB, M), 1)
        for group in range(groups):
            pick[group * SUB : (group + 1) * SUB, :] = jnp.where(
                numbers[:, group : group + 1] == lane, 1.0, 0.0
            ).astype(jnp.bfloat16)
        for side in range(2):
            chosen = jnp.dot(
                pick[...], natural[side], preferred_element_type=jnp.float32
            ).astype(jnp.bfloat16)
            for group in range(groups):
                outgoing[chunk, group, side * SUB : (side + 1) * SUB, :] = chosen[
                    group * SUB : (group + 1) * SUB, :
                ]
        for index in range(groups - 1):
            sending(chunk, index).start()

        @pl.when(stays)
        def _():
            keeping(chunk).start()

        @pl.when(jnp.logical_not(stays))
        def _():
            sending(chunk, groups - 1).start()

    def multiply(lhs, main_part, rest_part):
        depth = bands * LANES
        columns = main_part.shape[2]
        return jnp.dot(
            lhs[:, :depth], main_part.reshape(depth, columns), preferred_element_type=jnp.float32
        ) + jnp.dot(
            lhs[:, depth:], rest_part.reshape(bands * rest, columns), preferred_element_type=jnp.float32
        )

    def sums(tile, main_part, rest_part):
        window = base[tile]
        lhs = jnp.concatenate([ordered[window + slot] for slot in range(WINDOW)], axis=0)
        products = multiply(lhs, main_part, rest_part)
        columns = main_part.shape[2]
        ids = tile * TILE + lax.broadcasted_iota(jnp.int32, (SUB, columns), 1)
        held = jnp.zeros((SUB, columns), jnp.float32)
        for slot in range(WINDOW):
            held = jnp.where(
                ids >= starts[window + slot], products[slot * SUB : (slot + 1) * SUB, :], held
            )
        return jnp.where(ids >= starts[window + WINDOW], 0.0, held)

    phases = schedule(chunks * SUB, cols)
    bounds = [sum(phase < chunk for phase in phases[:tiles]) for chunk in range(chunks)] + [tiles]
    row_total = chunks * SUB * SUB
    waiting = []
    for chunk in range(chunks):
        for origin in range(origins):

            @pl.when(jnp.logical_not(stays & (place == origin)))
            def _():
                pltpu.make_async_remote_copy(
                    src_ref=received.at[chunk, origin],
                    dst_ref=received.at[chunk, origin],
                    send_sem=send_sem.at[chunk, 0],
                    recv_sem=recv_sem.at[chunk, origin],
                    device_id=(lat, fld, 1 - rep),
                    device_id_type=MESH,
                ).wait_recv()

        @pl.when(stays)
        def _():
            keeping(chunk).wait()

        quads = LANES // rest

        @pl.loop(0, bands // quads)
        def _(quad):
            for part in range(origins // bands):
                for level in range(levels):
                    for side in range(2):
                        row = (part * levels + level) * 2 + side
                        spread = pl.ds(row, SUB, stride=SUB)
                        from_rows = slice(side * SUB, (side + 1) * SUB)
                        pieces = []
                        for near in range(quads):
                            origin = part * bands + quad * quads + near
                            stage[quad * quads + near, spread, :] = received[
                                chunk, origin, from_rows, level * LANES : (level + 1) * LANES
                            ].astype(jnp.float32)
                            begin = levels * LANES + level * rest
                            pieces.append(
                                received[chunk, origin, from_rows, begin : begin + rest].astype(
                                    jnp.float32
                                )
                            )
                        stage[bands + quad, spread, :] = jnp.concatenate(pieces, axis=1)

        slots_here = slice(chunk * SUB, (chunk + 1) * SUB)
        for part in range(stage.shape[0]):
            ordered[slots_here, :, part * LANES : (part + 1) * LANES] = (
                stage[part].astype(jnp.bfloat16).reshape(SUB, SUB, LANES)
            )
        copy = pltpu.make_async_copy(ordered.at[slots_here], kept.at[slots_here], kept_sem.at[chunk])
        copy.start()
        waiting.append(copy)

        @pl.loop(bounds[chunk], bounds[chunk + 1])
        def _(tile):
            slot = lax.rem(tile, RING)
            for copy in ring_copies(tile, slot):
                copy.wait()
            held = sums(tile, ring_main[slot], ring_rest[slot])
            here = pl.ds(pl.multiple_of(tile * TILE, TILE), TILE)
            for level in range(total.shape[0]):
                total[level, :, here] = held[2 * level : 2 * level + 2, :]
            following = tile + RING

            @pl.when(following < tiles)
            def _():
                for copy in ring_copies(following, slot):
                    copy.start()

        if chunk == chunks - 1:
            for copy in tail_copies:
                copy.wait()
            held = sums(tiles, tail_main[...], tail_rest[...])
            for level in range(total.shape[0]):
                total[level, :, tiles * TILE : cols] = held[2 * level : 2 * level + 2, :]
        done = cols if chunk == chunks - 1 else bounds[chunk + 1] * TILE
        if done > bounds[chunk] * TILE:
            here = slice(bounds[chunk] * TILE, done)
            copy = pltpu.make_async_copy(total.at[:, :, here], out.at[:, :, here], out_sem.at[chunk])
            copy.start()
            waiting.append(copy)

    for side in range(2):

        @pl.when(exists[side])
        def _():
            halo_copy(side).wait_send()

    @pl.loop(0, chunks)
    def _(chunk):
        for index in range(groups - 1):
            sending(chunk, index).wait_send()

        @pl.when(jnp.logical_not(stays))
        def _():
            sending(chunk, groups - 1).wait_send()

    for copy in waiting:
        copy.wait()


def fused(dims, band, base, starts, order, field, wind_zonal, wind_merid, legendre):
    lat_size, fld_size, rep_size = dims
    levels, rows, length = field.shape
    groups = lat_size * fld_size
    slots = order.shape[0]
    chunks = slots // SUB
    bands = lat_size * rep_size
    origins = fld_size // rep_size * bands
    rest = rows - LANES
    parts = length // LANES
    width = pl.cdiv(levels * rows, LANES) * LANES
    depth = bands * rows
    cols = legendre.shape[2]
    tail = cols % TILE
    out_levels = origins // bands * levels
    matrix = jnp.asarray(folded_matrix(length))
    dma = pltpu.SemaphoreType.DMA
    smem = pl.BlockSpec(memory_space=pltpu.SMEM)
    vmem = pl.BlockSpec(memory_space=pltpu.VMEM)
    anywhere = pl.BlockSpec(memory_space=pltpu.HBM)
    return pl.pallas_call(
        functools.partial(fused_kernel, dims),
        out_shape=(
            jax.ShapeDtypeStruct((out_levels, 2, cols), jnp.float32),
            jax.ShapeDtypeStruct((slots, SUB, depth), jnp.bfloat16),
        ),
        in_specs=[smem, smem, smem, vmem] + [anywhere] * 5,
        out_specs=(anywhere, anywhere),
        scratch_shapes=[
            pltpu.VMEM((levels, parts, rows + 2 * PAD, LANES), jnp.float32),
            pltpu.VMEM((parts, rows + 2 * PAD, LANES), jnp.float32),
            pltpu.VMEM((levels, rows + 16, length), jnp.float32),
            pltpu.VMEM((levels, rows + 16, length), jnp.float32),
            pltpu.VMEM((2, 3, levels, 8, length), jnp.float32),
            pltpu.VMEM((2, parts, SUB, LANES), jnp.float32),
            pltpu.VMEM((2, parts, SUB, LANES), jnp.float32),
            pltpu.VMEM((2, width, length // 2), jnp.bfloat16),
            pltpu.VMEM((2 * M, length // 2), jnp.bfloat16),
            pltpu.VMEM((2, M, width), jnp.bfloat16),
            pltpu.VMEM((groups * SUB, M), jnp.bfloat16),
            pltpu.VMEM((chunks, groups, 2 * SUB, width), jnp.bfloat16),
            pltpu.VMEM((chunks, origins, 2 * SUB, width), jnp.bfloat16),
            pltpu.VMEM((depth // LANES, SUB * SUB, LANES), jnp.float32),
            pltpu.VMEM((slots, SUB, depth), jnp.bfloat16),
            pltpu.VMEM((RING, bands, LANES, TILE), jnp.bfloat16),
            pltpu.VMEM((RING, bands, rest, TILE), jnp.bfloat16),
            pltpu.VMEM((bands, LANES, tail), jnp.bfloat16),
            pltpu.VMEM((bands, rest, tail), jnp.bfloat16),
            pltpu.VMEM((out_levels, 2, cols), jnp.float32),
            dma((2, 3)),
            dma((levels, parts + 2)),
            dma,
            dma((2,)),
            dma((2,)),
            dma((chunks, groups)),
            dma((chunks, origins)),
            dma((chunks,)),
            dma((RING, 2)),
            dma((2,)),
            dma((chunks,)),
            dma((chunks,)),
        ],
        compiler_params=pltpu.CompilerParams(has_side_effects=True, vmem_limit_bytes=62 << 20),
    )(band, base, starts, order, field, wind_zonal, wind_merid, matrix, legendre)


def finish_kernel(
    rest, base, starts, extra, left, kept, legendre, partial, out, window_rows, main, tail, held, sem
):
    slots = kept.shape[0]
    bands = legendre.shape[0]
    cols = legendre.shape[2]
    depth = bands * LANES

    def moved(source, target):
        copy = pltpu.make_async_copy(source, target, sem)
        copy.start()
        copy.wait()

    @pl.when(left[0] > 0)
    def _():
        @pl.loop(0, extra.shape[0])
        def _(tile):
            @pl.loop(0, extra[tile])
            def _(turn):
                begin = base[tile] + WINDOW * (turn + 1)
                window = jnp.minimum(begin, slots - WINDOW)
                moved(kept.at[pl.ds(window, WINDOW)], window_rows)
                lhs = window_rows[...].reshape(WINDOW * SUB, kept.shape[2])

                @pl.loop(0, jnp.minimum(TILE, cols - tile * TILE) // LANES)
                def _(piece):
                    first = pl.multiple_of(tile * TILE + piece * LANES, LANES)
                    here = pl.ds(first, LANES)
                    moved(legendre.at[:, 0:LANES, here], main)
                    moved(legendre.at[:, LANES : LANES + rest, here], tail)
                    moved(out.at[:, :, here], held)
                    products = jnp.dot(
                        lhs[:, :depth], main[...].reshape(depth, LANES), preferred_element_type=jnp.float32
                    ) + jnp.dot(
                        lhs[:, depth:],
                        tail[...].reshape(bands * rest, LANES),
                        preferred_element_type=jnp.float32,
                    )
                    ids = first + lax.broadcasted_iota(jnp.int32, (SUB, LANES), 1)
                    more = jnp.zeros((SUB, LANES), jnp.float32)
                    for slot in range(WINDOW):
                        more = jnp.where(
                            ids >= starts[window + slot], products[slot * SUB : (slot + 1) * SUB, :], more
                        )
                    more = jnp.where(
                        (ids >= starts[begin]) & (ids < starts[window + WINDOW]), more, 0.0
                    )
                    for level in range(held.shape[0]):
                        held[level] += more[2 * level : 2 * level + 2, :]
                    moved(held, out.at[:, :, here])


def finish(base, starts, extra, left, kept, legendre, partial):
    bands, rows, _ = legendre.shape
    smem = pl.BlockSpec(memory_space=pltpu.SMEM)
    anywhere = pl.BlockSpec(memory_space=pltpu.HBM)
    return pl.pallas_call(
        functools.partial(finish_kernel, rows - LANES),
        out_shape=jax.ShapeDtypeStruct(partial.shape, partial.dtype),
        in_specs=[smem] * 4 + [anywhere] * 3,
        out_specs=anywhere,
        scratch_shapes=[
            pltpu.VMEM((WINDOW,) + kept.shape[1:], jnp.bfloat16),
            pltpu.VMEM((bands, LANES, LANES), jnp.bfloat16),
            pltpu.VMEM((bands, rows - LANES, LANES), jnp.bfloat16),
            pltpu.VMEM((partial.shape[0], 2, LANES), jnp.float32),
            pltpu.SemaphoreType.DMA,
        ],
        input_output_aliases={6: 0},
        compiler_params=pltpu.CompilerParams(vmem_limit_bytes=8 << 20),
    )(base, starts, extra, left, kept, legendre, partial)


def tables(waves, group, cols):
    groups, slots = waves.shape
    own = lax.dynamic_index_in_dim(waves, group, 0, keepdims=False)
    counts = jnp.where(own >= 0, M - own, 0)
    slot_ids = lax.broadcasted_iota(jnp.int32, (slots + WINDOW + 1, slots), 1)
    lower = slot_ids < lax.broadcasted_iota(jnp.int32, (slots + WINDOW + 1, slots), 0)
    starts = jnp.sum(jnp.where(lower, counts[None, :], 0), axis=1)
    phases = np.array(schedule(slots, cols), np.int32)
    edges = np.arange(phases.shape[0], dtype=np.int32)[:, None] * TILE
    first = jnp.sum((starts[None, 1 : slots + 1] <= edges).astype(jnp.int32), axis=1)
    begun = jnp.sum((starts[None, :slots] < np.minimum(edges + TILE, cols)).astype(jnp.int32), axis=1)
    base = jnp.minimum(first, (phases + 1) * SUB - WINDOW)
    extra = jnp.maximum(begun - base - 1, 0) // WINDOW
    order = jnp.where(waves >= 0, waves // 2 + waves % 2 * (M // 2), -1).T
    return base, starts, extra, jnp.sum(extra).reshape(1), order


def body(field, wind_zonal, wind_merid, band, waves, legendre):
    field_count, row_count, lon_count = field.shape
    lat_size = lax.axis_size("lat")
    fld_size = lax.axis_size("fld")
    rep_size = lax.axis_size("rep")
    first_row = (lax.axis_index("lat") * rep_size + lax.axis_index("rep")) * row_count
    slot_count = waves.shape[1]
    rest = row_count - LANES
    direct = (
        rest > 0
        and rest % SUB == 0
        and LANES % rest == 0
        and lat_size * rep_size % (LANES // rest) == 0
        and field_count * 4 <= SUB
        and slot_count % SUB == 0
        and lon_count == 2 * M
        and lon_count % (2 * LANES) == 0
        and legendre.shape[2] % LANES == 0
        and legendre.shape[2] > TILE
        and legendre.shape[2] % TILE > 0
        and rep_size == 2
        and fld_size % 2 == 0
        and fld_size // rep_size * field_count * 2 <= SUB
        and lat_size & (lat_size - 1) == 0
        and fld_size & (fld_size - 1) == 0
        and lat_size * fld_size <= 16
    )
    if direct:
        group = lax.axis_index("lat") * fld_size + lax.axis_index("fld")
        columns = legendre.reshape(lat_size * rep_size, row_count, legendre.shape[2])
        base, starts, extra, left, order = tables(waves, group, columns.shape[2])
        partial, kept = fused(
            (lat_size, fld_size, rep_size),
            band.T, base, starts, order, field, wind_zonal, wind_merid, columns,
        )
        return finish(base, starts, extra, left, kept, columns, partial)[None]
    bounds = lax.dynamic_slice_in_dim(band, lax.axis_index("fld") * field_count, field_count, 0)
    in_band = band_mask(bounds, first_row, row_count)
    padded = with_halo(field, ((("lat", "rep"), 1),), 1)
    first_section = field + in_band * tendency(
        field, padded[:, 2:], padded[:, :-2], wind_zonal, wind_merid
    )
    padded_section = with_halo(first_section, ((("lat", "rep"), 1),), 1)
    advected = 0.5 * (
        field
        + first_section
        + in_band
        * tendency(
            first_section, padded_section[:, 2:], padded_section[:, :-2], wind_zonal, wind_merid
        )
    )
    grid_low = advected.astype(jnp.bfloat16)
    spectra = jnp.dot(
        grid_low.reshape(field_count * row_count, lon_count),
        dft_matrix(lon_count, M),
        preferred_element_type=jnp.float32,
    ).astype(jnp.bfloat16)
    spectra = spectra.reshape(field_count, row_count, 2, M)
    wave_index = jnp.where(waves >= 0, waves, 0)
    picked = jnp.take(spectra, wave_index.reshape(-1), axis=3)
    picked = picked.reshape(field_count, row_count, 2, lat_size, fld_size, slot_count)
    outgoing = jnp.transpose(picked, (5, 2, 4, 0, 3, 1)).reshape(
        slot_count, 2, fld_size * field_count, lat_size * row_count
    )
    received = lax.all_to_all(
        lax.all_to_all(outgoing, "lat", split_axis=3, concat_axis=3, tiled=True),
        "fld",
        split_axis=2,
        concat_axis=2,
        tiled=True,
    )
    group = lax.axis_index("lat") * fld_size + lax.axis_index("fld")
    own_waves = lax.dynamic_index_in_dim(waves, group, 0, keepdims=False)
    counts = jnp.where(own_waves >= 0, M - own_waves, 0)
    offsets = jnp.cumsum(counts) - counts
    col_count = legendre.shape[2]
    col_ids = lax.broadcasted_iota(jnp.int32, (slot_count, col_count), 1)
    segments = ((col_ids >= offsets[:, None]) & (col_ids < (offsets + counts)[:, None])).astype(
        jnp.float32
    )
    total_fields = fld_size * field_count
    regrouped = lax.all_to_all(received, "rep", split_axis=2, concat_axis=3, tiled=True)
    half_fields = total_fields // rep_size
    ordered = regrouped.reshape(slot_count, 2, half_fields, rep_size, lat_size, row_count)
    ordered = jnp.transpose(ordered, (0, 1, 2, 4, 3, 5)).reshape(
        slot_count * 2 * half_fields, rep_size * lat_size * row_count
    )
    products = jnp.dot(ordered, legendre[0], preferred_element_type=jnp.float32)
    spectrum = jnp.einsum(
        "scfk,sk->fck", products.reshape(slot_count, 2, half_fields, col_count), segments
    )
    return spectrum[None]


def solution(mesh):
    placed = (
        P("fld", ("lat", "rep"), None),
        P("fld", ("lat", "rep"), None),
        P("fld", ("lat", "rep"), None),
        P(),
        P(),
        P(("lat", "fld"), None, None),
    )
    return jax.shard_map(
        body,
        mesh=mesh,
        in_specs=placed,
        out_specs=P(("lat", "fld"), "rep", None, None),
        check_vma=False,
    )
```

```python
import functools
import math

import jax
import jax.numpy as jnp
import ml_dtypes
import numpy as np
from jax import lax
from jax.experimental import pallas as pl
from jax.experimental.pallas import tpu as pltpu
from jax.sharding import PartitionSpec as P

M = 1280
LANES = 128
SUB = 16
GROUP = 8
AHEAD = 1
LIMIT = 60 << 20
TILE = 512
WINDOW = 8
RING = 10
PAD = 16
MESH = pl.DeviceIdType.MESH


def with_halo(value, sides, width):
    for axis, dim in sides:
        peers, length = (lax.axis_size(axis), value.shape[dim])
        up = [(i, (i + 1) % peers) for i in range(peers - 1)]
        down = [(j, i) for i, j in up]
        last = lax.slice_in_dim(value, length - width, length, axis=dim)
        first = lax.slice_in_dim(value, 0, width, axis=dim)
        before = lax.ppermute(last, axis, up)
        after = lax.ppermute(first, axis, down)
        value = jnp.concatenate([before, value, after], axis=dim)
    return value


def dft_matrix(lon_count, wave_count):
    lon_ids = lax.broadcasted_iota(jnp.int32, (lon_count, wave_count), 0)
    wave_ids = lax.broadcasted_iota(jnp.int32, (lon_count, wave_count), 1)
    angles = (lon_ids * wave_ids % lon_count).astype(jnp.float32) * (2.0 * math.pi / lon_count)
    scaling = 1.0 / math.sqrt(lon_count)
    return jnp.concatenate([jnp.cos(angles) * scaling, -jnp.sin(angles) * scaling], axis=1).astype(
        jnp.bfloat16
    )


def tendency(centre, above_row, below_row, zonal_wind, merid_wind):
    eastward = jnp.roll(centre, -1, axis=-1)
    westward = jnp.roll(centre, 1, axis=-1)
    return (
        -(zonal_wind + centre) * (eastward - westward) * 0.5
        - merid_wind * (above_row - below_row) * 0.5
    )


def band_mask(bounds, first_row, row_total):
    row_ids = first_row + lax.broadcasted_iota(jnp.int32, (1, row_total, 1), 1)
    lower_edge = bounds[:, 0][:, None, None]
    upper_edge = bounds[:, 1][:, None, None]
    return ((row_ids >= lower_edge) & (row_ids < upper_edge)).astype(jnp.float32)


def folded_matrix(lon_count):
    half = lon_count // 2
    waves = np.arange(M).reshape(M // 2, 2).T.reshape(2, 1, M // 2, 1)
    turns = (waves * np.arange(half)) % lon_count
    angles = turns * (2.0 * math.pi / lon_count)
    both = np.concatenate([np.cos(angles), -np.sin(angles)], axis=1) / math.sqrt(lon_count)
    return both.reshape(2 * M, half).astype(ml_dtypes.bfloat16)


def schedule(slots, cols):
    chunks = slots // GROUP
    phases = [0]
    for tile in range(cols // TILE):
        share = min(1.0, (tile + 1) * TILE / cols)
        needed = share * slots + 3.5 * math.sqrt(slots * share * (1.0 - share) / 3.0) + 1.0
        phase = min(chunks - 1, math.ceil(needed / GROUP) - 1)
        phases.append(max(phases[-1], phase))
    return phases[1:] + [chunks - 1]


def flipped(value, bits, size):
    result, bit = 0, 1
    while bit < size:
        digit = (value // bit) % 2
        result = result + bit * ((1 - digit) if bits & bit else digit)
        bit *= 2
    return result


def fused_kernel(
    dims,
    band,
    waves,
    field,
    zonal,
    merid,
    matrix_source,
    legendre,
    total,
    kept,
    table_out,
    table,
    numbers,
    entries,
    x,
    section,
    wind_zonal,
    wind_merid,
    edge,
    halo_out,
    halo_in,
    folded,
    matrix,
    natural,
    pick,
    outgoing,
    received,
    stage,
    ordered,
    ring_main,
    ring_rest,
    tail_main,
    tail_rest,
    edge_sem,
    field_sem,
    matrix_sem,
    halo_send,
    halo_recv,
    send_sem,
    recv_sem,
    own_sem,
    ring_sem,
    tail_sem,
    kept_sem,
    table_sem,
):
    lat_size, fld_size, rep_size = dims
    lat, fld, rep = lax.axis_index("lat"), lax.axis_index("fld"), lax.axis_index("rep")
    levels, rows, length = field.shape
    parts = length // LANES
    half = parts // 2
    groups = lat_size * fld_size
    chunks, origins = received.shape[0], received.shape[1]
    slots = chunks * GROUP
    bands = lat_size * rep_size
    rest = rows - LANES
    width = folded.shape[1]
    position = lat * rep_size + rep
    peers = bands
    waves_half = M // 2
    cols = legendre.shape[2]
    tiles = cols // TILE
    tail = cols - tiles * TILE
    start = position * rows

    edge_copies = []
    for side, first in enumerate((0, rows - 8)):
        for array, source in enumerate((field, zonal, merid)):
            edge_copies.append(
                pltpu.make_async_copy(
                    source.at[:, first : first + 8, :], edge.at[side, array], edge_sem.at[side, array]
                )
            )
    for copy in edge_copies:
        copy.start()

    def column_copy(level, part):
        return pltpu.make_async_copy(
            field.at[level, :, pl.ds(pl.multiple_of(part * LANES, LANES), LANES)],
            x.at[level, part, PAD : PAD + rows, :],
            field_sem.at[level, part],
        )

    def wind_copies(level):
        return (
            pltpu.make_async_copy(
                zonal.at[level], wind_zonal.at[level, 8 : 8 + rows, :], field_sem.at[level, parts]
            ),
            pltpu.make_async_copy(
                merid.at[level], wind_merid.at[level, 8 : 8 + rows, :], field_sem.at[level, parts + 1]
            ),
        )

    @pl.loop(0, levels)
    def _(level):
        @pl.loop(0, parts)
        def _(part):
            column_copy(level, part).start()

        for copy in wind_copies(level):
            copy.start()

    barrier = pltpu.get_barrier_semaphore()
    everyone = lat_size * fld_size * rep_size
    me = (lat * fld_size + fld) * rep_size + rep

    @pl.loop(1, everyone)
    def _(hop):
        peer = lax.rem(me + hop, everyone)
        pl.semaphore_signal(
            barrier,
            inc=1,
            device_id=(
                peer // (fld_size * rep_size),
                (peer // rep_size) % fld_size,
                peer % rep_size,
            ),
            device_id_type=MESH,
        )

    block_rows = waves_half // 2

    def matrix_copy(block):
        slot = lax.rem(block, matrix.shape[0])
        return pltpu.make_async_copy(
            matrix_source.at[pl.ds(pl.multiple_of(block * block_rows, SUB), block_rows), :],
            matrix.at[slot],
            matrix_sem.at[slot],
        )

    above = lax.rem(position + peers - 1, peers)
    below = lax.rem(position + 1, peers)

    def halo_copy(side):
        target = (above, below)[side]
        return pltpu.make_async_remote_copy(
            src_ref=halo_out.at[side],
            dst_ref=halo_in.at[1 - side],
            send_sem=halo_send.at[side],
            recv_sem=halo_recv.at[1 - side],
            device_id=(target // rep_size, fld, target % rep_size),
            device_id_type=MESH,
        )

    for block in range(matrix.shape[0]):
        matrix_copy(block).start()
    stage[...] = jnp.zeros(stage.shape, jnp.float32)
    filled = levels * rows
    folded[:, filled:width, :] = jnp.zeros((2, width - filled, folded.shape[2]), jnp.bfloat16)


    chosen = waves[...]
    numbers[...] = jnp.where(chosen >= 0, chosen // 2 + chosen % 2 * waves_half, -1).T
    mine = waves[pl.ds(lat * fld_size + fld, 1), :]
    counts = jnp.where(mine >= 0, M - mine, 0)
    slot_row = lax.broadcasted_iota(jnp.int32, (LANES, slots), 0)
    slot_lane = lax.broadcasted_iota(jnp.int32, (LANES, slots), 1)
    begins = jnp.sum(jnp.where(slot_lane < slot_row, counts, 0), axis=1, keepdims=True)
    ends = jnp.sum(jnp.where(slot_lane <= slot_row, counts, 0), axis=1, keepdims=True)
    real = lax.broadcasted_iota(jnp.int32, (LANES, LANES), 0) < slots
    lane = lax.broadcasted_iota(jnp.int32, (LANES, LANES), 1)
    row = lax.broadcasted_iota(jnp.int32, (LANES, LANES), 0)
    starts_row = jnp.sum(jnp.where(row == lane, begins, 0), axis=0, keepdims=True)
    first = jnp.sum(jnp.where(real & (ends <= lane * TILE), 1, 0), axis=0, keepdims=True)
    limit = jnp.minimum(lane * TILE + TILE, cols)
    begun = jnp.sum(jnp.where(real & (begins < limit), 1, 0), axis=0, keepdims=True)
    tile_lane = lane[0:1, :]
    phases = schedule(slots, cols)
    bounds = [sum(phase < chunk for phase in phases[:tiles]) for chunk in range(chunks)] + [tiles]
    ready = jnp.full((1, LANES), GROUP, jnp.int32)
    for chunk in range(1, chunks):
        ready += jnp.where(tile_lane >= bounds[chunk], GROUP, 0)
    ready = jnp.where(tile_lane >= tiles, slots, ready)
    base_row = jnp.minimum(first, ready - WINDOW)
    extra = lax.shift_right_arithmetic(jnp.maximum(begun - base_row - 1, 0), WINDOW.bit_length() - 1)
    extra = jnp.where(tile_lane <= tiles, extra, 0)
    left = jnp.broadcast_to(jnp.sum(extra, axis=1, keepdims=True), (1, LANES))
    entries[...] = jnp.concatenate(
        [base_row, starts_row, extra, left, jnp.zeros((4, LANES), jnp.int32)], axis=0
    )
    table_copies = (
        pltpu.make_async_copy(entries, table, table_sem.at[0]),
        pltpu.make_async_copy(entries, table_out, table_sem.at[1]),
    )
    for copy in table_copies:
        copy.start()

    exists = (position > 0, position < peers - 1)
    for copy in edge_copies:
        copy.wait()
    for part in range(parts):
        lanes = slice(part * LANES, (part + 1) * LANES)
        for level in range(levels):
            for side, (pair, single) in enumerate((((0, 2), (0, 1)), ((6, 8), (7, 8)))):
                halo_out[side, part, 2 * level : 2 * level + 2, :] = edge[
                    side, 0, level, pair[0] : pair[1], lanes
                ]
                for array in (1, 2):
                    row = (array + 1) * levels + level
                    halo_out[side, part, row : row + 1, :] = edge[
                        side, array, level, single[0] : single[1], lanes
                    ]
    def slopes(centre_of, next_of, previous_of, zonal_of, merid_of, scale, last_lane, first_lane):
        centres, easts, wests = {}, {}, {}

        def turn(part):
            if part not in centres:
                centres[part] = centre_of(part)
                easts[part] = pltpu.roll(centres[part], LANES - 1, axis=1)
                wests[part] = pltpu.roll(centres[part], 1, axis=1)

        def slope(part):
            after, before = (part + 1) % parts, (part - 1) % parts
            for needed in (part, after, before):
                turn(needed)
            east = jnp.where(last_lane, easts[after], easts[part])
            west = jnp.where(first_lane, wests[before], wests[part])
            centre = centres[part]
            return centre, scale * (
                (zonal_of(part) + centre) * (west - east)
                + merid_of(part) * (previous_of(part) - next_of(part))
            )

        return slope

    def scale_of(level, first_row, count):
        lower, upper = band[0, fld * levels + level], band[1, fld * levels + level]
        ids = start + first_row + lax.broadcasted_iota(jnp.int32, (count, LANES), 0)
        return jnp.where((ids >= lower) & (ids < upper), 0.5, 0.0)

    def edges_of(count):
        lane = lax.broadcasted_iota(jnp.int32, (count, LANES), 1)
        return lane == LANES - 1, lane == 0

    def greet():
        pl.semaphore_wait(barrier, everyone - 1)
        for side in range(2):

            @pl.when(exists[side])
            def _():
                halo_copy(side).start()

            @pl.when(jnp.logical_not(exists[side]))
            def _():
                halo_in[side] = jnp.zeros(halo_in.shape[1:], jnp.float32)

    def first_section(level, block):
        first = pl.multiple_of(block * 8, 8)
        at = pl.multiple_of(first + PAD - 8, 8)
        slope = slopes(
            lambda part: x[level, part, pl.ds(at, 8), :],
            lambda part: x[level, part, pl.ds(at + 1, 8), :],
            lambda part: x[level, part, pl.ds(at - 1, 8), :],
            lambda part: wind_zonal[level, pl.ds(first, 8), part * LANES : (part + 1) * LANES],
            lambda part: wind_merid[level, pl.ds(first, 8), part * LANES : (part + 1) * LANES],
            scale_of(level, first - 8, 8),
            *edges_of(8),
        )
        for part in range(parts):
            centre, change = slope(part)
            section[level, part, pl.ds(at, 8), :] = centre + change

    @pl.loop(0, levels)
    def _(level):
        @pl.loop(0, parts)
        def _(part):
            column_copy(level, part).wait()

        for copy in wind_copies(level):
            copy.wait()

        @pl.loop(2, rows // 8)
        def _(block):
            first_section(level, block)

        @pl.when(level == 0)
        def _():
            greet()

    for side in range(2):

        @pl.when(exists[side])
        def _():
            halo_copy(1 - side).wait_recv()

    for part in range(parts):
        lanes = slice(part * LANES, (part + 1) * LANES)
        for level in range(levels):
            pair = slice(2 * level, 2 * level + 2)
            x[level, part, PAD - 2 : PAD, :] = halo_in[0, part, pair, :]
            x[level, part, PAD + rows : PAD + rows + 2, :] = halo_in[1, part, pair, :]
            for array, wind in ((1, wind_zonal), (2, wind_merid)):
                row = (array + 1) * levels + level
                wind[level, 7:8, lanes] = halo_in[0, part, row : row + 1, :]
                wind[level, 8 + rows : 9 + rows, lanes] = halo_in[1, part, row : row + 1, :]

    @pl.loop(0, levels)
    def _(level):
        @pl.loop(0, 4)
        def _(side):
            first_section(level, side % 2 + side // 2 * (rows // 8))

        @pl.loop(0, rows // SUB)
        def _(block):
            first = pl.multiple_of(block * SUB, SUB)
            at = pl.multiple_of(first + PAD, SUB)
            wind_at = pl.multiple_of(first + 8, 8)
            slope = slopes(
                lambda part: section[level, part, pl.ds(at, SUB), :],
                lambda part: section[level, part, pl.ds(at + 1, SUB), :],
                lambda part: section[level, part, pl.ds(at - 1, SUB), :],
                lambda part: wind_zonal[level, pl.ds(wind_at, SUB), part * LANES : (part + 1) * LANES],
                lambda part: wind_merid[level, pl.ds(wind_at, SUB), part * LANES : (part + 1) * LANES],
                scale_of(level, first, SUB),
                *edges_of(SUB),
            )

            def advected(part):
                centre, change = slope(part)
                return 0.5 * (x[level, part, pl.ds(at, SUB), :] + centre + change)

            late = first // LANES
            goes = (1 - late) * (level * LANES + first) + late * (
                levels * LANES + level * rest + first - LANES
            )
            goes = pl.ds(pl.multiple_of(goes, SUB), SUB)
            for part in range(half):
                near, far = advected(part), advected(part + half)
                lanes = slice(part * LANES, (part + 1) * LANES)
                folded[0, goes, lanes] = (near + far).astype(jnp.bfloat16)
                folded[1, goes, lanes] = (near - far).astype(jnp.bfloat16)

    def ring_copies(tile, slot):
        columns = pl.ds(pl.multiple_of(tile * TILE, TILE), TILE)
        return (
            pltpu.make_async_copy(
                legendre.at[:, 0:LANES, columns], ring_main.at[slot], ring_sem.at[slot, 0]
            ),
            pltpu.make_async_copy(
                legendre.at[:, LANES:rows, columns], ring_rest.at[slot], ring_sem.at[slot, 1]
            ),
        )

    for tile in range(min(RING, tiles)):
        for copy in ring_copies(tile, tile):
            copy.start()
    tail_columns = slice(tiles * TILE, cols)
    tail_copies = (
        pltpu.make_async_copy(legendre.at[:, 0:LANES, tail_columns], tail_main, tail_sem.at[0]),
        pltpu.make_async_copy(legendre.at[:, LANES:rows, tail_columns], tail_rest, tail_sem.at[1]),
    )
    for copy in tail_copies:
        copy.start()


    @pl.loop(0, 8)
    def _(block):
        parity, side, piece = block // 4, (block // 2) % 2, block % 2
        matrix_copy(block).wait()
        slot = lax.rem(block, matrix.shape[0])
        there = pl.ds(pl.multiple_of(parity * waves_half + piece * block_rows, SUB), block_rows)
        natural[side, there, :] = lax.dot_general(
            matrix[slot], folded[parity], (((1,), (1,)), ((), ())), preferred_element_type=jnp.float32
        ).astype(jnp.bfloat16)
        following = block + matrix.shape[0]

        @pl.when(following < 8)
        def _():
            matrix_copy(following).start()

    half_flds = fld_size // rep_size
    to_rep = fld // half_flds
    place = ((fld % half_flds) * lat_size + lat) * rep_size + rep
    own = lat * fld_size + fld
    stays = to_rep == rep
    hops = [(i, j) for i in range(lat_size - 1, -1, -1) for j in range(fld_size - 1, -1, -1)]

    def sending(chunk, index):
        far_lat = flipped(lat, hops[index][0], lat_size)
        far_fld = flipped(fld, hops[index][1], fld_size)
        return pltpu.make_async_remote_copy(
            src_ref=outgoing.at[chunk, far_lat * fld_size + far_fld],
            dst_ref=received.at[chunk, place],
            send_sem=send_sem.at[chunk, index],
            recv_sem=recv_sem.at[chunk, place],
            device_id=(far_lat, far_fld, to_rep),
            device_id_type=MESH,
        )

    def keeping(chunk):
        return pltpu.make_async_copy(
            outgoing.at[chunk, own], received.at[chunk, place], own_sem.at[chunk]
        )

    pairs = SUB // GROUP

    def send_pair(several):
        near = numbers[several * SUB : (several + 1) * SUB, :]
        lane = lax.broadcasted_iota(jnp.int32, (GROUP, M), 1)
        for piece in range(pairs):
            for group in range(groups):
                at = (piece * groups + group) * GROUP
                column = near[piece * GROUP : (piece + 1) * GROUP, group : group + 1]
                pick[at : at + GROUP, :] = jnp.where(column == lane, 1.0, 0.0)
        picked = pick[...].astype(jnp.bfloat16)
        sides = [
            jnp.dot(picked, natural[side], preferred_element_type=jnp.float32) for side in range(2)
        ]
        for piece in range(pairs):
            chunk = several * pairs + piece
            for group in range(groups):
                at = (piece * groups + group) * GROUP
                outgoing[chunk, group] = jnp.concatenate(
                    [side[at : at + GROUP, :] for side in sides], axis=0
                ).astype(jnp.bfloat16)
            for index in range(groups - 1):
                sending(chunk, index).start()

            @pl.when(stays)
            def _():
                keeping(chunk).start()

            @pl.when(jnp.logical_not(stays))
            def _():
                sending(chunk, groups - 1).start()

    def multiply(lhs, main_part, rest_part):
        depth = bands * LANES
        columns = main_part.shape[2]
        return jnp.dot(
            lhs[:, :depth], main_part.reshape(depth, columns), preferred_element_type=jnp.float32
        ) + jnp.dot(
            lhs[:, depth:], rest_part.reshape(bands * rest, columns), preferred_element_type=jnp.float32
        )

    def sums(tile, main_part, rest_part):
        window = table[0, tile]
        lhs = jnp.concatenate([ordered[window + slot] for slot in range(WINDOW)], axis=0)
        products = multiply(lhs, main_part, rest_part)
        columns = main_part.shape[2]
        ids = tile * TILE + lax.broadcasted_iota(jnp.int32, (SUB, columns), 1)
        held = jnp.zeros((SUB, columns), jnp.float32)
        for slot in range(WINDOW):
            held = jnp.where(
                ids >= table[1, window + slot], products[slot * SUB : (slot + 1) * SUB, :], held
            )
        return jnp.where(ids >= table[1, window + WINDOW], 0.0, held)

    for copy in table_copies:
        copy.wait()
    waiting = []
    for several in range(min(AHEAD, chunks // pairs)):
        send_pair(several)
    for chunk in range(chunks):
        for origin in range(origins):

            @pl.when(jnp.logical_not(stays & (place == origin)))
            def _():
                pltpu.make_async_remote_copy(
                    src_ref=received.at[chunk, origin],
                    dst_ref=received.at[chunk, origin],
                    send_sem=send_sem.at[chunk, 0],
                    recv_sem=recv_sem.at[chunk, origin],
                    device_id=(lat, fld, 1 - rep),
                    device_id_type=MESH,
                ).wait_recv()

        @pl.when(stays)
        def _():
            keeping(chunk).wait()

        if chunk % pairs == 0 and chunk // pairs + AHEAD < chunks // pairs:
            send_pair(chunk // pairs + AHEAD)
        quads = LANES // rest

        @pl.loop(0, bands // quads)
        def _(quad):
            for part in range(origins // bands):
                for level in range(levels):
                    for side in range(2):
                        row = (part * levels + level) * 2 + side
                        spread = pl.ds(row, GROUP, stride=SUB)
                        from_rows = slice(side * GROUP, (side + 1) * GROUP)
                        pieces = []
                        for near in range(quads):
                            origin = part * bands + quad * quads + near
                            stage[quad * quads + near, spread, :] = received[
                                chunk, origin, :, level * LANES : (level + 1) * LANES
                            ].astype(jnp.float32)[from_rows]
                            begin = levels * LANES + level * rest
                            pieces.append(
                                received[chunk, origin, :, begin : begin + rest].astype(jnp.float32)[
                                    from_rows
                                ]
                            )
                        stage[bands + quad, spread, :] = jnp.concatenate(pieces, axis=1)

        slots_here = slice(chunk * GROUP, (chunk + 1) * GROUP)
        for part in range(stage.shape[0]):
            ordered[slots_here, :, part * LANES : (part + 1) * LANES] = (
                stage[part].astype(jnp.bfloat16).reshape(GROUP, SUB, LANES)
            )
        copy = pltpu.make_async_copy(ordered.at[slots_here], kept.at[slots_here], kept_sem.at[chunk])
        copy.start()
        waiting.append(copy)

        @pl.loop(bounds[chunk], bounds[chunk + 1])
        def _(tile):
            slot = lax.rem(tile, RING)
            for copy in ring_copies(tile, slot):
                copy.wait()
            held = sums(tile, ring_main[slot], ring_rest[slot])
            here = pl.ds(pl.multiple_of(tile * TILE, TILE), TILE)
            for level in range(total.shape[0]):
                total[level, :, here] = held[2 * level : 2 * level + 2, :]
            following = tile + RING

            @pl.when(following < tiles)
            def _():
                for copy in ring_copies(following, slot):
                    copy.start()

        if chunk == chunks - 1:
            for copy in tail_copies:
                copy.wait()
            held = sums(tiles, tail_main[...], tail_rest[...])
            for level in range(total.shape[0]):
                total[level, :, tiles * TILE : cols] = held[2 * level : 2 * level + 2, :]

    for side in range(2):

        @pl.when(exists[side])
        def _():
            halo_copy(side).wait_send()

    @pl.loop(0, chunks)
    def _(chunk):
        for index in range(groups - 1):
            sending(chunk, index).wait_send()

        @pl.when(jnp.logical_not(stays))
        def _():
            sending(chunk, groups - 1).wait_send()

    for copy in waiting:
        copy.wait()


def fused(dims, band, waves, field, wind_zonal, wind_merid, legendre):
    lat_size, fld_size, rep_size = dims
    levels, rows, length = field.shape
    groups = lat_size * fld_size
    slots = waves.shape[1]
    chunks = slots // GROUP
    bands = lat_size * rep_size
    origins = fld_size // rep_size * bands
    rest = rows - LANES
    parts = length // LANES
    width = pl.cdiv(levels * rows, LANES) * LANES
    depth = bands * rows
    cols = legendre.shape[2]
    tail = cols % TILE
    out_levels = origins // bands * levels
    matrix = jnp.asarray(folded_matrix(length))
    dma = pltpu.SemaphoreType.DMA
    smem = pl.BlockSpec(memory_space=pltpu.SMEM)
    vmem = pl.BlockSpec(memory_space=pltpu.VMEM)
    anywhere = pl.BlockSpec(memory_space=pltpu.HBM)
    return pl.pallas_call(
        functools.partial(fused_kernel, dims),
        out_shape=(
            jax.ShapeDtypeStruct((out_levels, 2, cols), jnp.float32),
            jax.ShapeDtypeStruct((slots, SUB, depth), jnp.bfloat16),
            jax.ShapeDtypeStruct((8, LANES), jnp.int32),
        ),
        in_specs=[smem, vmem] + [anywhere] * 5,
        out_specs=(vmem, anywhere, anywhere),
        scratch_shapes=[
            pltpu.SMEM((8, LANES), jnp.int32),
            pltpu.VMEM((slots, groups), jnp.int32),
            pltpu.VMEM((8, LANES), jnp.int32),
            pltpu.VMEM((levels, parts, rows + 2 * PAD, LANES), jnp.float32),
            pltpu.VMEM((levels, parts, rows + 2 * PAD, LANES), jnp.float32),
            pltpu.VMEM((levels, rows + 16, length), jnp.float32),
            pltpu.VMEM((levels, rows + 16, length), jnp.float32),
            pltpu.VMEM((2, 3, levels, 8, length), jnp.float32),
            pltpu.VMEM((2, parts, SUB, LANES), jnp.float32),
            pltpu.VMEM((2, parts, SUB, LANES), jnp.float32),
            pltpu.VMEM((2, width, length // 2), jnp.bfloat16),
            pltpu.VMEM((3, M // 4, length // 2), jnp.bfloat16),
            pltpu.VMEM((2, M, width), jnp.bfloat16),
            pltpu.VMEM((groups * SUB, M), jnp.float32),
            pltpu.VMEM((chunks, groups, 2 * GROUP, width), jnp.bfloat16),
            pltpu.VMEM((chunks, origins, 2 * GROUP, width), jnp.bfloat16),
            pltpu.VMEM((depth // LANES, GROUP * SUB, LANES), jnp.float32),
            pltpu.VMEM((slots, SUB, depth), jnp.bfloat16),
            pltpu.VMEM((RING, bands, LANES, TILE), jnp.bfloat16),
            pltpu.VMEM((RING, bands, rest, TILE), jnp.bfloat16),
            pltpu.VMEM((bands, LANES, tail), jnp.bfloat16),
            pltpu.VMEM((bands, rest, tail), jnp.bfloat16),
            dma((2, 3)),
            dma((levels, parts + 2)),
            dma((3,)),
            dma((2,)),
            dma((2,)),
            dma((chunks, groups)),
            dma((chunks, origins)),
            dma((chunks,)),
            dma((RING, 2)),
            dma((2,)),
            dma((chunks,)),
            dma((2,)),
        ],
        compiler_params=pltpu.CompilerParams(
            collective_id=0, has_side_effects=True, vmem_limit_bytes=LIMIT
        ),
    )(band, waves, field, wind_zonal, wind_merid, matrix, legendre)


def finish_kernel(
    rest, table, partial, kept, legendre, out, window_rows, main, tail, held, sem
):
    slots = kept.shape[0]
    bands = legendre.shape[0]
    cols = legendre.shape[2]
    depth = bands * LANES

    def moved(source, target):
        copy = pltpu.make_async_copy(source, target, sem)
        copy.start()
        copy.wait()

    moved(partial, out)

    @pl.when(table[3, 0] > 0)
    def _():
        @pl.loop(0, pl.cdiv(cols, TILE))
        def _(tile):
            @pl.loop(0, table[2, tile])
            def _(turn):
                begin = table[0, tile] + WINDOW * (turn + 1)
                window = jnp.minimum(begin, slots - WINDOW)
                moved(kept.at[pl.ds(window, WINDOW)], window_rows)
                lhs = window_rows[...].reshape(WINDOW * SUB, kept.shape[2])

                @pl.loop(0, jnp.minimum(TILE, cols - tile * TILE) // LANES)
                def _(piece):
                    first = pl.multiple_of(tile * TILE + piece * LANES, LANES)
                    here = pl.ds(first, LANES)
                    moved(legendre.at[:, 0:LANES, here], main)
                    moved(legendre.at[:, LANES : LANES + rest, here], tail)
                    moved(out.at[:, :, here], held)
                    products = jnp.dot(
                        lhs[:, :depth], main[...].reshape(depth, LANES), preferred_element_type=jnp.float32
                    ) + jnp.dot(
                        lhs[:, depth:],
                        tail[...].reshape(bands * rest, LANES),
                        preferred_element_type=jnp.float32,
                    )
                    ids = first + lax.broadcasted_iota(jnp.int32, (SUB, LANES), 1)
                    more = jnp.zeros((SUB, LANES), jnp.float32)
                    for slot in range(WINDOW):
                        more = jnp.where(
                            ids >= table[1, window + slot], products[slot * SUB : (slot + 1) * SUB, :], more
                        )
                    more = jnp.where(
                        (ids >= table[1, begin]) & (ids < table[1, window + WINDOW]), more, 0.0
                    )
                    for level in range(held.shape[0]):
                        held[level] += more[2 * level : 2 * level + 2, :]
                    moved(held, out.at[:, :, here])


def finish(table, partial, kept, legendre):
    bands, rows, _ = legendre.shape
    smem = pl.BlockSpec(memory_space=pltpu.SMEM)
    vmem = pl.BlockSpec(memory_space=pltpu.VMEM)
    anywhere = pl.BlockSpec(memory_space=pltpu.HBM)
    return pl.pallas_call(
        functools.partial(finish_kernel, rows - LANES),
        out_shape=jax.ShapeDtypeStruct(partial.shape, partial.dtype),
        in_specs=[smem, vmem, anywhere, anywhere],
        out_specs=anywhere,
        scratch_shapes=[
            pltpu.VMEM((WINDOW,) + kept.shape[1:], jnp.bfloat16),
            pltpu.VMEM((bands, LANES, LANES), jnp.bfloat16),
            pltpu.VMEM((bands, rows - LANES, LANES), jnp.bfloat16),
            pltpu.VMEM((partial.shape[0], 2, LANES), jnp.float32),
            pltpu.SemaphoreType.DMA,
        ],
        compiler_params=pltpu.CompilerParams(vmem_limit_bytes=LIMIT),
    )(table, partial, kept, legendre)


def body(field, wind_zonal, wind_merid, band, waves, legendre):
    field_count, row_count, lon_count = field.shape
    lat_size = lax.axis_size("lat")
    fld_size = lax.axis_size("fld")
    rep_size = lax.axis_size("rep")
    first_row = (lax.axis_index("lat") * rep_size + lax.axis_index("rep")) * row_count
    slot_count = waves.shape[1]
    rest = row_count - LANES
    direct = (
        rest > 0
        and rest % SUB == 0
        and LANES % rest == 0
        and lat_size * rep_size % (LANES // rest) == 0
        and field_count * 4 <= SUB
        and slot_count % SUB == 0
        and slot_count + WINDOW < LANES
        and legendre.shape[2] // TILE < LANES
        and lon_count == 2 * M
        and lon_count % (2 * LANES) == 0
        and legendre.shape[2] % LANES == 0
        and legendre.shape[2] > TILE
        and legendre.shape[2] % TILE > 0
        and rep_size == 2
        and fld_size % 2 == 0
        and fld_size // rep_size * field_count * 2 <= SUB
        and lat_size & (lat_size - 1) == 0
        and fld_size & (fld_size - 1) == 0
        and lat_size * fld_size <= 16
    )
    if direct:
        columns = legendre.reshape(lat_size * rep_size, row_count, legendre.shape[2])
        partial, kept, table = fused(
            (lat_size, fld_size, rep_size),
            band.T, waves, field, wind_zonal, wind_merid, columns,
        )
        return finish(table, partial, kept, columns)[None]
    bounds = lax.dynamic_slice_in_dim(band, lax.axis_index("fld") * field_count, field_count, 0)
    in_band = band_mask(bounds, first_row, row_count)
    padded = with_halo(field, ((("lat", "rep"), 1),), 1)
    first_section = field + in_band * tendency(
        field, padded[:, 2:], padded[:, :-2], wind_zonal, wind_merid
    )
    padded_section = with_halo(first_section, ((("lat", "rep"), 1),), 1)
    advected = 0.5 * (
        field
        + first_section
        + in_band
        * tendency(
            first_section, padded_section[:, 2:], padded_section[:, :-2], wind_zonal, wind_merid
        )
    )
    grid_low = advected.astype(jnp.bfloat16)
    spectra = jnp.dot(
        grid_low.reshape(field_count * row_count, lon_count),
        dft_matrix(lon_count, M),
        preferred_element_type=jnp.float32,
    ).astype(jnp.bfloat16)
    spectra = spectra.reshape(field_count, row_count, 2, M)
    wave_index = jnp.where(waves >= 0, waves, 0)
    picked = jnp.take(spectra, wave_index.reshape(-1), axis=3)
    picked = picked.reshape(field_count, row_count, 2, lat_size, fld_size, slot_count)
    outgoing = jnp.transpose(picked, (5, 2, 4, 0, 3, 1)).reshape(
        slot_count, 2, fld_size * field_count, lat_size * row_count
    )
    received = lax.all_to_all(
        lax.all_to_all(outgoing, "lat", split_axis=3, concat_axis=3, tiled=True),
        "fld",
        split_axis=2,
        concat_axis=2,
        tiled=True,
    )
    group = lax.axis_index("lat") * fld_size + lax.axis_index("fld")
    own_waves = lax.dynamic_index_in_dim(waves, group, 0, keepdims=False)
    counts = jnp.where(own_waves >= 0, M - own_waves, 0)
    offsets = jnp.cumsum(counts) - counts
    col_count = legendre.shape[2]
    col_ids = lax.broadcasted_iota(jnp.int32, (slot_count, col_count), 1)
    segments = ((col_ids >= offsets[:, None]) & (col_ids < (offsets + counts)[:, None])).astype(
        jnp.float32
    )
    total_fields = fld_size * field_count
    regrouped = lax.all_to_all(received, "rep", split_axis=2, concat_axis=3, tiled=True)
    half_fields = total_fields // rep_size
    ordered = regrouped.reshape(slot_count, 2, half_fields, rep_size, lat_size, row_count)
    ordered = jnp.transpose(ordered, (0, 1, 2, 4, 3, 5)).reshape(
        slot_count * 2 * half_fields, rep_size * lat_size * row_count
    )
    products = jnp.dot(ordered, legendre[0], preferred_element_type=jnp.float32)
    spectrum = jnp.einsum(
        "scfk,sk->fck", products.reshape(slot_count, 2, half_fields, col_count), segments
    )
    return spectrum[None]


def solution(mesh):
    placed = (
        P("fld", ("lat", "rep"), None),
        P("fld", ("lat", "rep"), None),
        P("fld", ("lat", "rep"), None),
        P(),
        P(),
        P(("lat", "fld"), None, None),
    )
    return jax.shard_map(
        body,
        mesh=mesh,
        in_specs=placed,
        out_specs=P(("lat", "fld"), "rep", None, None),
        check_vma=False,
    )
```

```python
import functools
import math

import jax
import jax.numpy as jnp
import ml_dtypes
import numpy as np
from jax import lax
from jax.experimental import pallas as pl
from jax.experimental.pallas import tpu as pltpu
from jax.sharding import PartitionSpec as P

M = 1280
LANES = 128
SUB = 16
GROUP = 8
AHEAD = 1
LIMIT = 60 << 20
TILE = 512
WIDE = 2 * TILE
WINDOW = 8
RING = 5
PAD = 16
MESH = pl.DeviceIdType.MESH


def with_halo(value, sides, width):
    for axis, dim in sides:
        peers, length = (lax.axis_size(axis), value.shape[dim])
        up = [(i, (i + 1) % peers) for i in range(peers - 1)]
        down = [(j, i) for i, j in up]
        last = lax.slice_in_dim(value, length - width, length, axis=dim)
        first = lax.slice_in_dim(value, 0, width, axis=dim)
        before = lax.ppermute(last, axis, up)
        after = lax.ppermute(first, axis, down)
        value = jnp.concatenate([before, value, after], axis=dim)
    return value


def dft_matrix(lon_count, wave_count):
    lon_ids = lax.broadcasted_iota(jnp.int32, (lon_count, wave_count), 0)
    wave_ids = lax.broadcasted_iota(jnp.int32, (lon_count, wave_count), 1)
    angles = (lon_ids * wave_ids % lon_count).astype(jnp.float32) * (2.0 * math.pi / lon_count)
    scaling = 1.0 / math.sqrt(lon_count)
    return jnp.concatenate([jnp.cos(angles) * scaling, -jnp.sin(angles) * scaling], axis=1).astype(
        jnp.bfloat16
    )


def tendency(centre, above_row, below_row, zonal_wind, merid_wind):
    eastward = jnp.roll(centre, -1, axis=-1)
    westward = jnp.roll(centre, 1, axis=-1)
    return (
        -(zonal_wind + centre) * (eastward - westward) * 0.5
        - merid_wind * (above_row - below_row) * 0.5
    )


def band_mask(bounds, first_row, row_total):
    row_ids = first_row + lax.broadcasted_iota(jnp.int32, (1, row_total, 1), 1)
    lower_edge = bounds[:, 0][:, None, None]
    upper_edge = bounds[:, 1][:, None, None]
    return ((row_ids >= lower_edge) & (row_ids < upper_edge)).astype(jnp.float32)


def folded_matrix(lon_count):
    half = lon_count // 2
    waves = np.arange(M).reshape(M // 2, 2).T.reshape(2, 1, M // 2, 1)
    turns = (waves * np.arange(half)) % lon_count
    angles = turns * (2.0 * math.pi / lon_count)
    both = np.concatenate([np.cos(angles), -np.sin(angles)], axis=1) / math.sqrt(lon_count)
    both = both.reshape(2, 2, 2, M // 4, half).transpose(0, 2, 1, 3, 4)
    return both.reshape(2 * M, half).astype(ml_dtypes.bfloat16)


def schedule(slots, cols):
    chunks = slots // GROUP
    phases = [0]
    for tile in range(cols // TILE):
        share = min(1.0, (tile + 1) * TILE / cols)
        needed = share * slots + 3.5 * math.sqrt(slots * share * (1.0 - share) / 3.0) + 1.0
        phase = min(chunks - 1, math.ceil(needed / GROUP) - 1)
        phases.append(max(phases[-1], phase))
    phases = phases[1:]
    return [phases[tile // 2 * 2 + 1] for tile in range(len(phases))] + [chunks - 1]


def flipped(value, bits, size):
    result, bit = 0, 1
    while bit < size:
        digit = (value // bit) % 2
        result = result + bit * ((1 - digit) if bits & bit else digit)
        bit *= 2
    return result


def fused_kernel(
    dims,
    band,
    waves,
    field,
    zonal,
    merid,
    matrix_source,
    legendre,
    total,
    kept,
    table_out,
    table,
    numbers,
    entries,
    x,
    section,
    wind_zonal,
    wind_merid,
    edge,
    halo_out,
    halo_in,
    folded,
    matrix,
    natural_first,
    natural,
    pick,
    outgoing_first,
    received_first,
    outgoing,
    received,
    stage,
    ordered,
    ring_main,
    ring_rest,
    tail_main,
    tail_rest,
    edge_sem,
    field_sem,
    matrix_sem,
    halo_send,
    halo_recv,
    send_sem,
    recv_sem,
    own_sem,
    send_first,
    recv_first,
    own_first,
    ring_sem,
    tail_sem,
    kept_sem,
    table_sem,
):
    lat_size, fld_size, rep_size = dims
    lat, fld, rep = lax.axis_index("lat"), lax.axis_index("fld"), lax.axis_index("rep")
    levels, rows, length = field.shape
    parts = length // LANES
    half = parts // 2
    groups = lat_size * fld_size
    chunks, origins = received.shape[0], received.shape[1]
    slots = chunks * GROUP
    bands = lat_size * rep_size
    rest = rows - LANES
    width = folded.shape[1]
    position = lat * rep_size + rep
    peers = bands
    waves_half = M // 2
    cols = legendre.shape[2]
    tiles = cols // TILE
    steps = cols // WIDE
    tail = cols - tiles * TILE
    start = position * rows

    edge_copies = []
    for side, first in enumerate((0, rows - 8)):
        for array, source in enumerate((field, zonal, merid)):
            edge_copies.append(
                pltpu.make_async_copy(
                    source.at[:, first : first + 8, :], edge.at[side, array], edge_sem.at[side, array]
                )
            )
    for copy in edge_copies:
        copy.start()

    def column_copy(level, part):
        return pltpu.make_async_copy(
            field.at[level, :, pl.ds(pl.multiple_of(part * LANES, LANES), LANES)],
            x.at[level, part, PAD : PAD + rows, :],
            field_sem.at[level, part],
        )

    def wind_copies(level):
        return (
            pltpu.make_async_copy(
                zonal.at[level], wind_zonal.at[level, 8 : 8 + rows, :], field_sem.at[level, parts]
            ),
            pltpu.make_async_copy(
                merid.at[level], wind_merid.at[level, 8 : 8 + rows, :], field_sem.at[level, parts + 1]
            ),
        )

    @pl.loop(0, levels)
    def _(level):
        @pl.loop(0, parts)
        def _(part):
            column_copy(level, part).start()

        for copy in wind_copies(level):
            copy.start()

    barrier = pltpu.get_barrier_semaphore()
    everyone = lat_size * fld_size * rep_size
    me = (lat * fld_size + fld) * rep_size + rep

    @pl.loop(1, everyone)
    def _(hop):
        peer = lax.rem(me + hop, everyone)
        pl.semaphore_signal(
            barrier,
            inc=1,
            device_id=(
                peer // (fld_size * rep_size),
                (peer // rep_size) % fld_size,
                peer % rep_size,
            ),
            device_id_type=MESH,
        )

    block_rows = waves_half // 2

    def matrix_copy(block):
        slot = lax.rem(block, matrix.shape[0])
        return pltpu.make_async_copy(
            matrix_source.at[pl.ds(pl.multiple_of(block % 8 * block_rows, SUB), block_rows), :],
            matrix.at[slot],
            matrix_sem.at[slot],
        )

    above = lax.rem(position + peers - 1, peers)
    below = lax.rem(position + 1, peers)

    def halo_copy(side):
        target = (above, below)[side]
        return pltpu.make_async_remote_copy(
            src_ref=halo_out.at[side],
            dst_ref=halo_in.at[1 - side],
            send_sem=halo_send.at[side],
            recv_sem=halo_recv.at[1 - side],
            device_id=(target // rep_size, fld, target % rep_size),
            device_id_type=MESH,
        )

    for block in range(matrix.shape[0]):
        matrix_copy(block).start()
    stage[...] = jnp.zeros(stage.shape, jnp.float32)
    filled = levels * rows
    folded[:, filled:width, :] = jnp.zeros((2, width - filled, folded.shape[2]), jnp.bfloat16)


    chosen = waves[...]
    numbers[...] = jnp.where(chosen >= 0, chosen // 2 + chosen % 2 * waves_half, -1).T
    mine = waves[pl.ds(lat * fld_size + fld, 1), :]
    counts = jnp.where(mine >= 0, M - mine, 0)
    slot_row = lax.broadcasted_iota(jnp.int32, (LANES, slots), 0)
    slot_lane = lax.broadcasted_iota(jnp.int32, (LANES, slots), 1)
    begins = jnp.sum(jnp.where(slot_lane < slot_row, counts, 0), axis=1, keepdims=True)
    ends = jnp.sum(jnp.where(slot_lane <= slot_row, counts, 0), axis=1, keepdims=True)
    real = lax.broadcasted_iota(jnp.int32, (LANES, LANES), 0) < slots
    lane = lax.broadcasted_iota(jnp.int32, (LANES, LANES), 1)
    row = lax.broadcasted_iota(jnp.int32, (LANES, LANES), 0)
    starts_row = jnp.sum(jnp.where(row == lane, begins, 0), axis=0, keepdims=True)
    first = jnp.sum(jnp.where(real & (ends <= lane * TILE), 1, 0), axis=0, keepdims=True)
    limit = jnp.minimum(lane * TILE + TILE, cols)
    begun = jnp.sum(jnp.where(real & (begins < limit), 1, 0), axis=0, keepdims=True)
    tile_lane = lane[0:1, :]
    phases = schedule(slots, cols)
    bounds = [sum(phase < chunk for phase in phases[:tiles]) for chunk in range(chunks)] + [tiles]
    ready = jnp.full((1, LANES), GROUP, jnp.int32)
    for chunk in range(1, chunks):
        ready += jnp.where(tile_lane >= bounds[chunk], GROUP, 0)
    ready = jnp.where(tile_lane >= tiles, slots, ready)
    base_row = jnp.minimum(first, ready - WINDOW)
    extra = lax.shift_right_arithmetic(jnp.maximum(begun - base_row - 1, 0), WINDOW.bit_length() - 1)
    extra = jnp.where(tile_lane <= tiles, extra, 0)
    left = jnp.broadcast_to(jnp.sum(extra, axis=1, keepdims=True), (1, LANES))
    entries[...] = jnp.concatenate(
        [base_row, starts_row, extra, left, jnp.zeros((4, LANES), jnp.int32)], axis=0
    )
    table_copies = (
        pltpu.make_async_copy(entries, table, table_sem.at[0]),
        pltpu.make_async_copy(entries, table_out, table_sem.at[1]),
    )
    for copy in table_copies:
        copy.start()

    exists = (position > 0, position < peers - 1)
    for copy in edge_copies:
        copy.wait()
    for part in range(parts):
        lanes = slice(part * LANES, (part + 1) * LANES)
        for level in range(levels):
            for side, (pair, single) in enumerate((((0, 2), (0, 1)), ((6, 8), (7, 8)))):
                halo_out[side, part, 2 * level : 2 * level + 2, :] = edge[
                    side, 0, level, pair[0] : pair[1], lanes
                ]
                for array in (1, 2):
                    row = (array + 1) * levels + level
                    halo_out[side, part, row : row + 1, :] = edge[
                        side, array, level, single[0] : single[1], lanes
                    ]
    def slopes(centre_of, next_of, previous_of, zonal_of, merid_of, scale, last_lane, first_lane):
        centres, easts, wests = {}, {}, {}

        def turn(part):
            if part not in centres:
                centres[part] = centre_of(part)
                easts[part] = pltpu.roll(centres[part], LANES - 1, axis=1)
                wests[part] = pltpu.roll(centres[part], 1, axis=1)

        def slope(part):
            after, before = (part + 1) % parts, (part - 1) % parts
            for needed in (part, after, before):
                turn(needed)
            east = jnp.where(last_lane, easts[after], easts[part])
            west = jnp.where(first_lane, wests[before], wests[part])
            centre = centres[part]
            return centre, scale * (
                (zonal_of(part) + centre) * (west - east)
                + merid_of(part) * (previous_of(part) - next_of(part))
            )

        return slope

    def scale_of(level, first_row, count):
        lower, upper = band[0, fld * levels + level], band[1, fld * levels + level]
        ids = start + first_row + lax.broadcasted_iota(jnp.int32, (count, LANES), 0)
        return jnp.where((ids >= lower) & (ids < upper), 0.5, 0.0)

    def edges_of(count):
        lane = lax.broadcasted_iota(jnp.int32, (count, LANES), 1)
        return lane == LANES - 1, lane == 0

    def greet():
        pl.semaphore_wait(barrier, everyone - 1)
        for side in range(2):

            @pl.when(exists[side])
            def _():
                halo_copy(side).start()

            @pl.when(jnp.logical_not(exists[side]))
            def _():
                halo_in[side] = jnp.zeros(halo_in.shape[1:], jnp.float32)

    def first_section(level, block):
        first = pl.multiple_of(block * 8, 8)
        at = pl.multiple_of(first + PAD - 8, 8)
        slope = slopes(
            lambda part: x[level, part, pl.ds(at, 8), :],
            lambda part: x[level, part, pl.ds(at + 1, 8), :],
            lambda part: x[level, part, pl.ds(at - 1, 8), :],
            lambda part: wind_zonal[level, pl.ds(first, 8), part * LANES : (part + 1) * LANES],
            lambda part: wind_merid[level, pl.ds(first, 8), part * LANES : (part + 1) * LANES],
            scale_of(level, first - 8, 8),
            *edges_of(8),
        )
        for part in range(parts):
            centre, change = slope(part)
            section[level, part, pl.ds(at, 8), :] = centre + change

    @pl.loop(0, levels)
    def _(level):
        @pl.loop(0, parts)
        def _(part):
            column_copy(level, part).wait()

        for copy in wind_copies(level):
            copy.wait()

        @pl.loop(2, rows // 8)
        def _(block):
            first_section(level, block)

        @pl.when(level == 0)
        def _():
            greet()

    for side in range(2):

        @pl.when(exists[side])
        def _():
            halo_copy(1 - side).wait_recv()

    for part in range(parts):
        lanes = slice(part * LANES, (part + 1) * LANES)
        for level in range(levels):
            pair = slice(2 * level, 2 * level + 2)
            x[level, part, PAD - 2 : PAD, :] = halo_in[0, part, pair, :]
            x[level, part, PAD + rows : PAD + rows + 2, :] = halo_in[1, part, pair, :]
            for array, wind in ((1, wind_zonal), (2, wind_merid)):
                row = (array + 1) * levels + level
                wind[level, 7:8, lanes] = halo_in[0, part, row : row + 1, :]
                wind[level, 8 + rows : 9 + rows, lanes] = halo_in[1, part, row : row + 1, :]

    def boundary_rows(level):
        @pl.loop(0, 4)
        def _(side):
            first_section(level, side % 2 + side // 2 * (rows // 8))

    def second_section(level):
        @pl.loop(0, rows // SUB)
        def _(block):
            first = pl.multiple_of(block * SUB, SUB)
            at = pl.multiple_of(first + PAD, SUB)
            wind_at = pl.multiple_of(first + 8, 8)
            slope = slopes(
                lambda part: section[level, part, pl.ds(at, SUB), :],
                lambda part: section[level, part, pl.ds(at + 1, SUB), :],
                lambda part: section[level, part, pl.ds(at - 1, SUB), :],
                lambda part: wind_zonal[level, pl.ds(wind_at, SUB), part * LANES : (part + 1) * LANES],
                lambda part: wind_merid[level, pl.ds(wind_at, SUB), part * LANES : (part + 1) * LANES],
                scale_of(level, first, SUB),
                *edges_of(SUB),
            )

            def advected(part):
                centre, change = slope(part)
                return 0.5 * (x[level, part, pl.ds(at, SUB), :] + centre + change)

            late = first // LANES
            goes = (1 - late) * (level * LANES + first) + late * (
                levels * LANES + level * rest + first - LANES
            )
            goes = pl.ds(pl.multiple_of(goes, SUB), SUB)
            for part in range(half):
                near, far = advected(part), advected(part + half)
                lanes = slice(part * LANES, (part + 1) * LANES)
                folded[0, goes, lanes] = (near + far).astype(jnp.bfloat16)
                folded[1, goes, lanes] = (near - far).astype(jnp.bfloat16)

    boundary_rows(0)
    second_section(0)
    def fetch(block):
        @pl.when(block < 16)
        def _():
            matrix_copy(block).start()

    def product(slot, values):
        return lax.dot_general(
            matrix[slot], values, (((1,), (1,)), ((), ())), preferred_element_type=jnp.float32
        ).astype(jnp.bfloat16)

    @pl.loop(0, 4)
    def _(quarter):
        for side in range(2):
            there = pl.ds(pl.multiple_of(quarter * block_rows, SUB), block_rows)
            matrix_copy(2 * quarter + side).wait()
            slot = lax.rem(2 * quarter + side, matrix.shape[0])
            natural_first[there, side * LANES : (side + 1) * LANES] = product(
                slot, folded[quarter // 2, 0:LANES, :]
            )
            fetch(2 * quarter + side + matrix.shape[0])

    half_flds = fld_size // rep_size
    to_rep = fld // half_flds
    place = ((fld % half_flds) * lat_size + lat) * rep_size + rep
    own = lat * fld_size + fld
    stays = to_rep == rep
    hops = [(i, j) for i in range(lat_size - 1, -1, -1) for j in range(fld_size - 1, -1, -1)]

    def sending(chunk, index):
        far_lat = flipped(lat, hops[index][0], lat_size)
        far_fld = flipped(fld, hops[index][1], fld_size)
        return pltpu.make_async_remote_copy(
            src_ref=outgoing.at[chunk, far_lat * fld_size + far_fld],
            dst_ref=received.at[chunk, place],
            send_sem=send_sem.at[chunk, index],
            recv_sem=recv_sem.at[chunk, place],
            device_id=(far_lat, far_fld, to_rep),
            device_id_type=MESH,
        )

    def keeping(chunk):
        return pltpu.make_async_copy(
            outgoing.at[chunk, own], received.at[chunk, place], own_sem.at[chunk]
        )

    pairs = SUB // GROUP

    def picked_rows(several):
        near = numbers[pl.ds(pl.multiple_of(several * SUB, SUB), SUB), :]
        lane = lax.broadcasted_iota(jnp.int32, (GROUP, M), 1)
        for piece in range(pairs):
            for group in range(groups):
                at = (piece * groups + group) * GROUP
                column = near[piece * GROUP : (piece + 1) * GROUP, group : group + 1]
                pick[at : at + GROUP, :] = jnp.where(column == lane, 1.0, 0.0)
        return pick[...].astype(jnp.bfloat16)

    def send_pair(several):
        picked = picked_rows(several)
        sides = [
            jnp.dot(picked, natural[side], preferred_element_type=jnp.float32) for side in range(2)
        ]
        for piece in range(pairs):
            chunk = several * pairs + piece
            for group in range(groups):
                at = (piece * groups + group) * GROUP
                outgoing[chunk, group] = jnp.concatenate(
                    [side[at : at + GROUP, :] for side in sides], axis=0
                ).astype(jnp.bfloat16)
            for index in range(groups - 1):
                sending(chunk, index).start()

            @pl.when(stays)
            def _():
                keeping(chunk).start()

            @pl.when(jnp.logical_not(stays))
            def _():
                sending(chunk, groups - 1).start()

    def sending_first(index):
        far_lat = flipped(lat, hops[index][0], lat_size)
        far_fld = flipped(fld, hops[index][1], fld_size)
        return pltpu.make_async_remote_copy(
            src_ref=outgoing_first.at[far_lat * fld_size + far_fld],
            dst_ref=received_first.at[place],
            send_sem=send_first.at[index],
            recv_sem=recv_first.at[place],
            device_id=(far_lat, far_fld, to_rep),
            device_id_type=MESH,
        )

    keeping_first = pltpu.make_async_copy(
        outgoing_first.at[own], received_first.at[place], own_first
    )

    @pl.loop(0, chunks // pairs)
    def _(several):
        both = jnp.dot(picked_rows(several), natural_first[...], preferred_element_type=jnp.float32)
        for piece in range(pairs):
            for group in range(groups):
                at = (piece * groups + group) * GROUP
                outgoing_first[group, several * pairs + piece] = jnp.concatenate(
                    [both[at : at + GROUP, 0:LANES], both[at : at + GROUP, LANES : 2 * LANES]], axis=0
                ).astype(jnp.bfloat16)

    for index in range(groups - 1):
        sending_first(index).start()

    @pl.when(stays)
    def _():
        keeping_first.start()

    @pl.when(jnp.logical_not(stays))
    def _():
        sending_first(groups - 1).start()

    def ring_copies(tile, slot):
        columns = pl.ds(pl.multiple_of(tile * WIDE, WIDE), WIDE)
        return (
            pltpu.make_async_copy(
                legendre.at[:, 0:LANES, columns], ring_main.at[slot], ring_sem.at[slot, 0]
            ),
            pltpu.make_async_copy(
                legendre.at[:, LANES:rows, columns], ring_rest.at[slot], ring_sem.at[slot, 1]
            ),
        )

    for tile in range(min(RING, steps)):
        for copy in ring_copies(tile, tile):
            copy.start()
    tail_columns = slice(tiles * TILE, cols)
    tail_copies = (
        pltpu.make_async_copy(legendre.at[:, 0:LANES, tail_columns], tail_main, tail_sem.at[0]),
        pltpu.make_async_copy(legendre.at[:, LANES:rows, tail_columns], tail_rest, tail_sem.at[1]),
    )
    for copy in tail_copies:
        copy.start()


    @pl.loop(1, levels)
    def _(level):
        boundary_rows(level)
        second_section(level)

    @pl.loop(0, 4)
    def _(quarter):
        for side in range(2):
            block = 8 + 2 * quarter + side
            there = pl.ds(pl.multiple_of(quarter * block_rows, SUB), block_rows)
            matrix_copy(block).wait()
            natural[side, there, :] = product(
                lax.rem(block, matrix.shape[0]), folded[quarter // 2, LANES:width, :]
            )
            fetch(block + matrix.shape[0])

    def multiply(lhs, main_part, rest_part):
        depth = bands * LANES
        columns = main_part.shape[2]
        return jnp.dot(
            lhs[:, :depth], main_part.reshape(depth, columns), preferred_element_type=jnp.float32
        ) + jnp.dot(
            lhs[:, depth:], rest_part.reshape(bands * rest, columns), preferred_element_type=jnp.float32
        )

    def sums(tile, main_part, rest_part):
        window = table[0, tile]
        lhs = jnp.concatenate([ordered[window + slot] for slot in range(WINDOW)], axis=0)
        products = multiply(lhs, main_part, rest_part)
        columns = main_part.shape[2]
        ids = tile * TILE + lax.broadcasted_iota(jnp.int32, (SUB, columns), 1)
        held = jnp.zeros((SUB, columns), jnp.float32)
        for slot in range(WINDOW):
            held = jnp.where(
                ids >= table[1, window + slot], products[slot * SUB : (slot + 1) * SUB, :], held
            )
        return jnp.where(ids >= table[1, window + WINDOW], 0.0, held)

    for copy in table_copies:
        copy.wait()
    waiting = []
    for several in range(min(AHEAD, chunks // pairs)):
        send_pair(several)
    for origin in range(origins):

        @pl.when(jnp.logical_not(stays & (place == origin)))
        def _():
            pltpu.make_async_remote_copy(
                src_ref=received_first.at[origin],
                dst_ref=received_first.at[origin],
                send_sem=send_first.at[0],
                recv_sem=recv_first.at[origin],
                device_id=(lat, fld, 1 - rep),
                device_id_type=MESH,
            ).wait_recv()

    @pl.when(stays)
    def _():
        keeping_first.wait()

    for chunk in range(chunks):
        for origin in range(origins):

            @pl.when(jnp.logical_not(stays & (place == origin)))
            def _():
                pltpu.make_async_remote_copy(
                    src_ref=received.at[chunk, origin],
                    dst_ref=received.at[chunk, origin],
                    send_sem=send_sem.at[chunk, 0],
                    recv_sem=recv_sem.at[chunk, origin],
                    device_id=(lat, fld, 1 - rep),
                    device_id_type=MESH,
                ).wait_recv()

        @pl.when(stays)
        def _():
            keeping(chunk).wait()

        if chunk % pairs == 0 and chunk // pairs + AHEAD < chunks // pairs:
            send_pair(chunk // pairs + AHEAD)
        quads = LANES // rest

        @pl.loop(0, bands // quads)
        def _(quad):
            for part in range(origins // bands):
                for level in range(levels):
                    for side in range(2):
                        row = (part * levels + level) * 2 + side
                        spread = pl.ds(row, GROUP, stride=SUB)
                        from_rows = slice(side * GROUP, (side + 1) * GROUP)
                        pieces = []
                        for near in range(quads):
                            origin = part * bands + quad * quads + near
                            if level == 0:
                                whole = received_first[origin, chunk]
                            else:
                                whole = received[chunk, origin, :, (level - 1) * LANES : level * LANES]
                            stage[quad * quads + near, spread, :] = whole.astype(jnp.float32)[from_rows]
                            begin = (levels - 1) * LANES + level * rest
                            pieces.append(
                                received[chunk, origin, :, begin : begin + rest].astype(jnp.float32)[
                                    from_rows
                                ]
                            )
                        stage[bands + quad, spread, :] = jnp.concatenate(pieces, axis=1)

        slots_here = slice(chunk * GROUP, (chunk + 1) * GROUP)
        for part in range(stage.shape[0]):
            ordered[slots_here, :, part * LANES : (part + 1) * LANES] = (
                stage[part].astype(jnp.bfloat16).reshape(GROUP, SUB, LANES)
            )
        copy = pltpu.make_async_copy(ordered.at[slots_here], kept.at[slots_here], kept_sem.at[chunk])
        copy.start()
        waiting.append(copy)

        @pl.loop(bounds[chunk] // 2, bounds[chunk + 1] // 2)
        def _(tile):
            slot = lax.rem(tile, RING)
            for copy in ring_copies(tile, slot):
                copy.wait()
            for side in range(2):
                columns = slice(side * TILE, (side + 1) * TILE)
                held = sums(
                    2 * tile + side, ring_main[slot, :, :, columns], ring_rest[slot, :, :, columns]
                )
                here = pl.ds(pl.multiple_of(tile * WIDE + side * TILE, TILE), TILE)
                for level in range(total.shape[0]):
                    total[level, :, here] = held[2 * level : 2 * level + 2, :]
            following = tile + RING

            @pl.when(following < steps)
            def _():
                for copy in ring_copies(following, slot):
                    copy.start()

        if chunk == chunks - 1:
            for copy in tail_copies:
                copy.wait()
            held = sums(tiles, tail_main[...], tail_rest[...])
            for level in range(total.shape[0]):
                total[level, :, tiles * TILE : cols] = held[2 * level : 2 * level + 2, :]

    for side in range(2):

        @pl.when(exists[side])
        def _():
            halo_copy(side).wait_send()

    for index in range(groups - 1):
        sending_first(index).wait_send()

    @pl.when(jnp.logical_not(stays))
    def _():
        sending_first(groups - 1).wait_send()

    @pl.loop(0, chunks)
    def _(chunk):
        for index in range(groups - 1):
            sending(chunk, index).wait_send()

        @pl.when(jnp.logical_not(stays))
        def _():
            sending(chunk, groups - 1).wait_send()

    for copy in waiting:
        copy.wait()


def fused(dims, band, waves, field, wind_zonal, wind_merid, legendre):
    lat_size, fld_size, rep_size = dims
    levels, rows, length = field.shape
    groups = lat_size * fld_size
    slots = waves.shape[1]
    chunks = slots // GROUP
    bands = lat_size * rep_size
    origins = fld_size // rep_size * bands
    rest = rows - LANES
    parts = length // LANES
    width = pl.cdiv(levels * rows, LANES) * LANES
    depth = bands * rows
    cols = legendre.shape[2]
    tail = cols % TILE
    out_levels = origins // bands * levels
    matrix = jnp.asarray(folded_matrix(length))
    dma = pltpu.SemaphoreType.DMA
    smem = pl.BlockSpec(memory_space=pltpu.SMEM)
    vmem = pl.BlockSpec(memory_space=pltpu.VMEM)
    anywhere = pl.BlockSpec(memory_space=pltpu.HBM)
    return pl.pallas_call(
        functools.partial(fused_kernel, dims),
        out_shape=(
            jax.ShapeDtypeStruct((out_levels, 2, cols), jnp.float32),
            jax.ShapeDtypeStruct((slots, SUB, depth), jnp.bfloat16),
            jax.ShapeDtypeStruct((8, LANES), jnp.int32),
        ),
        in_specs=[smem, vmem] + [anywhere] * 5,
        out_specs=(vmem, anywhere, anywhere),
        scratch_shapes=[
            pltpu.SMEM((8, LANES), jnp.int32),
            pltpu.VMEM((slots, groups), jnp.int32),
            pltpu.VMEM((8, LANES), jnp.int32),
            pltpu.VMEM((levels, parts, rows + 2 * PAD, LANES), jnp.float32),
            pltpu.VMEM((levels, parts, rows + 2 * PAD, LANES), jnp.float32),
            pltpu.VMEM((levels, rows + 16, length), jnp.float32),
            pltpu.VMEM((levels, rows + 16, length), jnp.float32),
            pltpu.VMEM((2, 3, levels, 8, length), jnp.float32),
            pltpu.VMEM((2, parts, SUB, LANES), jnp.float32),
            pltpu.VMEM((2, parts, SUB, LANES), jnp.float32),
            pltpu.VMEM((2, width, length // 2), jnp.bfloat16),
            pltpu.VMEM((3, M // 4, length // 2), jnp.bfloat16),
            pltpu.VMEM((M, 2 * LANES), jnp.bfloat16),
            pltpu.VMEM((2, M, width - LANES), jnp.bfloat16),
            pltpu.VMEM((groups * SUB, M), jnp.float32),
            pltpu.VMEM((groups, chunks, 2 * GROUP, LANES), jnp.bfloat16),
            pltpu.VMEM((origins, chunks, 2 * GROUP, LANES), jnp.bfloat16),
            pltpu.VMEM((chunks, groups, 2 * GROUP, width - LANES), jnp.bfloat16),
            pltpu.VMEM((chunks, origins, 2 * GROUP, width - LANES), jnp.bfloat16),
            pltpu.VMEM((depth // LANES, GROUP * SUB, LANES), jnp.float32),
            pltpu.VMEM((slots, SUB, depth), jnp.bfloat16),
            pltpu.VMEM((RING, bands, LANES, WIDE), jnp.bfloat16),
            pltpu.VMEM((RING, bands, rest, WIDE), jnp.bfloat16),
            pltpu.VMEM((bands, LANES, tail), jnp.bfloat16),
            pltpu.VMEM((bands, rest, tail), jnp.bfloat16),
            dma((2, 3)),
            dma((levels, parts + 2)),
            dma((3,)),
            dma((2,)),
            dma((2,)),
            dma((chunks, groups)),
            dma((chunks, origins)),
            dma((chunks,)),
            dma((groups,)),
            dma((origins,)),
            dma,
            dma((RING, 2)),
            dma((2,)),
            dma((chunks,)),
            dma((2,)),
        ],
        compiler_params=pltpu.CompilerParams(
            collective_id=0, has_side_effects=True, vmem_limit_bytes=LIMIT
        ),
    )(band, waves, field, wind_zonal, wind_merid, matrix, legendre)


def finish_kernel(
    rest, table, partial, kept, legendre, out, window_rows, main, tail, held, sem
):
    slots = kept.shape[0]
    bands = legendre.shape[0]
    cols = legendre.shape[2]
    depth = bands * LANES

    def moved(source, target):
        copy = pltpu.make_async_copy(source, target, sem)
        copy.start()
        copy.wait()

    moved(partial, out)

    @pl.when(table[3, 0] > 0)
    def _():
        @pl.loop(0, pl.cdiv(cols, TILE))
        def _(tile):
            @pl.loop(0, table[2, tile])
            def _(turn):
                begin = table[0, tile] + WINDOW * (turn + 1)
                window = jnp.minimum(begin, slots - WINDOW)
                moved(kept.at[pl.ds(window, WINDOW)], window_rows)
                lhs = window_rows[...].reshape(WINDOW * SUB, kept.shape[2])

                @pl.loop(0, jnp.minimum(TILE, cols - tile * TILE) // LANES)
                def _(piece):
                    first = pl.multiple_of(tile * TILE + piece * LANES, LANES)
                    here = pl.ds(first, LANES)
                    moved(legendre.at[:, 0:LANES, here], main)
                    moved(legendre.at[:, LANES : LANES + rest, here], tail)
                    moved(out.at[:, :, here], held)
                    products = jnp.dot(
                        lhs[:, :depth], main[...].reshape(depth, LANES), preferred_element_type=jnp.float32
                    ) + jnp.dot(
                        lhs[:, depth:],
                        tail[...].reshape(bands * rest, LANES),
                        preferred_element_type=jnp.float32,
                    )
                    ids = first + lax.broadcasted_iota(jnp.int32, (SUB, LANES), 1)
                    more = jnp.zeros((SUB, LANES), jnp.float32)
                    for slot in range(WINDOW):
                        more = jnp.where(
                            ids >= table[1, window + slot], products[slot * SUB : (slot + 1) * SUB, :], more
                        )
                    more = jnp.where(
                        (ids >= table[1, begin]) & (ids < table[1, window + WINDOW]), more, 0.0
                    )
                    for level in range(held.shape[0]):
                        held[level] += more[2 * level : 2 * level + 2, :]
                    moved(held, out.at[:, :, here])


def finish(table, partial, kept, legendre):
    bands, rows, _ = legendre.shape
    smem = pl.BlockSpec(memory_space=pltpu.SMEM)
    vmem = pl.BlockSpec(memory_space=pltpu.VMEM)
    anywhere = pl.BlockSpec(memory_space=pltpu.HBM)
    return pl.pallas_call(
        functools.partial(finish_kernel, rows - LANES),
        out_shape=jax.ShapeDtypeStruct(partial.shape, partial.dtype),
        in_specs=[smem, vmem, anywhere, anywhere],
        out_specs=anywhere,
        scratch_shapes=[
            pltpu.VMEM((WINDOW,) + kept.shape[1:], jnp.bfloat16),
            pltpu.VMEM((bands, LANES, LANES), jnp.bfloat16),
            pltpu.VMEM((bands, rows - LANES, LANES), jnp.bfloat16),
            pltpu.VMEM((partial.shape[0], 2, LANES), jnp.float32),
            pltpu.SemaphoreType.DMA,
        ],
        compiler_params=pltpu.CompilerParams(vmem_limit_bytes=LIMIT),
    )(table, partial, kept, legendre)


def body(field, wind_zonal, wind_merid, band, waves, legendre):
    field_count, row_count, lon_count = field.shape
    lat_size = lax.axis_size("lat")
    fld_size = lax.axis_size("fld")
    rep_size = lax.axis_size("rep")
    first_row = (lax.axis_index("lat") * rep_size + lax.axis_index("rep")) * row_count
    slot_count = waves.shape[1]
    rest = row_count - LANES
    direct = (
        rest > 0
        and rest % SUB == 0
        and LANES % rest == 0
        and lat_size * rep_size % (LANES // rest) == 0
        and field_count * 4 <= SUB
        and slot_count % SUB == 0
        and slot_count + WINDOW < LANES
        and legendre.shape[2] // TILE < LANES
        and lon_count == 2 * M
        and lon_count % (2 * LANES) == 0
        and legendre.shape[2] % LANES == 0
        and legendre.shape[2] > WIDE
        and 0 < legendre.shape[2] % WIDE < TILE
        and rep_size == 2
        and fld_size % 2 == 0
        and fld_size // rep_size * field_count * 2 <= SUB
        and lat_size & (lat_size - 1) == 0
        and fld_size & (fld_size - 1) == 0
        and lat_size * fld_size <= 16
    )
    if direct:
        columns = legendre.reshape(lat_size * rep_size, row_count, legendre.shape[2])
        partial, kept, table = fused(
            (lat_size, fld_size, rep_size),
            band.T, waves, field, wind_zonal, wind_merid, columns,
        )
        return finish(table, partial, kept, columns)[None]
    bounds = lax.dynamic_slice_in_dim(band, lax.axis_index("fld") * field_count, field_count, 0)
    in_band = band_mask(bounds, first_row, row_count)
    padded = with_halo(field, ((("lat", "rep"), 1),), 1)
    first_section = field + in_band * tendency(
        field, padded[:, 2:], padded[:, :-2], wind_zonal, wind_merid
    )
    padded_section = with_halo(first_section, ((("lat", "rep"), 1),), 1)
    advected = 0.5 * (
        field
        + first_section
        + in_band
        * tendency(
            first_section, padded_section[:, 2:], padded_section[:, :-2], wind_zonal, wind_merid
        )
    )
    grid_low = advected.astype(jnp.bfloat16)
    spectra = jnp.dot(
        grid_low.reshape(field_count * row_count, lon_count),
        dft_matrix(lon_count, M),
        preferred_element_type=jnp.float32,
    ).astype(jnp.bfloat16)
    spectra = spectra.reshape(field_count, row_count, 2, M)
    wave_index = jnp.where(waves >= 0, waves, 0)
    picked = jnp.take(spectra, wave_index.reshape(-1), axis=3)
    picked = picked.reshape(field_count, row_count, 2, lat_size, fld_size, slot_count)
    outgoing = jnp.transpose(picked, (5, 2, 4, 0, 3, 1)).reshape(
        slot_count, 2, fld_size * field_count, lat_size * row_count
    )
    received = lax.all_to_all(
        lax.all_to_all(outgoing, "lat", split_axis=3, concat_axis=3, tiled=True),
        "fld",
        split_axis=2,
        concat_axis=2,
        tiled=True,
    )
    group = lax.axis_index("lat") * fld_size + lax.axis_index("fld")
    own_waves = lax.dynamic_index_in_dim(waves, group, 0, keepdims=False)
    counts = jnp.where(own_waves >= 0, M - own_waves, 0)
    offsets = jnp.cumsum(counts) - counts
    col_count = legendre.shape[2]
    col_ids = lax.broadcasted_iota(jnp.int32, (slot_count, col_count), 1)
    segments = ((col_ids >= offsets[:, None]) & (col_ids < (offsets + counts)[:, None])).astype(
        jnp.float32
    )
    total_fields = fld_size * field_count
    regrouped = lax.all_to_all(received, "rep", split_axis=2, concat_axis=3, tiled=True)
    half_fields = total_fields // rep_size
    ordered = regrouped.reshape(slot_count, 2, half_fields, rep_size, lat_size, row_count)
    ordered = jnp.transpose(ordered, (0, 1, 2, 4, 3, 5)).reshape(
        slot_count * 2 * half_fields, rep_size * lat_size * row_count
    )
    products = jnp.dot(ordered, legendre[0], preferred_element_type=jnp.float32)
    spectrum = jnp.einsum(
        "scfk,sk->fck", products.reshape(slot_count, 2, half_fields, col_count), segments
    )
    return spectrum[None]


def solution(mesh):
    placed = (
        P("fld", ("lat", "rep"), None),
        P("fld", ("lat", "rep"), None),
        P("fld", ("lat", "rep"), None),
        P(),
        P(),
        P(("lat", "fld"), None, None),
    )
    return jax.shard_map(
        body,
        mesh=mesh,
        in_specs=placed,
        out_specs=P(("lat", "fld"), "rep", None, None),
        check_vma=False,
    )
```

```python
import functools
import math

import jax
import jax.numpy as jnp
import ml_dtypes
import numpy as np
from jax import lax
from jax.experimental import pallas as pl
from jax.experimental.pallas import tpu as pltpu
from jax.sharding import PartitionSpec as P

M = 1280
LANES = 128
SUB = 16
GROUP = 8
AHEAD = 1
LIMIT = 60 << 20
TILE = 512
WIDE = 2 * TILE
WINDOW = 8
RING = 4
PAD = 16
MESH = pl.DeviceIdType.MESH


def with_halo(value, sides, width):
    for axis, dim in sides:
        peers, length = (lax.axis_size(axis), value.shape[dim])
        up = [(i, (i + 1) % peers) for i in range(peers - 1)]
        down = [(j, i) for i, j in up]
        last = lax.slice_in_dim(value, length - width, length, axis=dim)
        first = lax.slice_in_dim(value, 0, width, axis=dim)
        before = lax.ppermute(last, axis, up)
        after = lax.ppermute(first, axis, down)
        value = jnp.concatenate([before, value, after], axis=dim)
    return value


def dft_matrix(lon_count, wave_count):
    lon_ids = lax.broadcasted_iota(jnp.int32, (lon_count, wave_count), 0)
    wave_ids = lax.broadcasted_iota(jnp.int32, (lon_count, wave_count), 1)
    angles = (lon_ids * wave_ids % lon_count).astype(jnp.float32) * (2.0 * math.pi / lon_count)
    scaling = 1.0 / math.sqrt(lon_count)
    return jnp.concatenate([jnp.cos(angles) * scaling, -jnp.sin(angles) * scaling], axis=1).astype(
        jnp.bfloat16
    )


def tendency(centre, above_row, below_row, zonal_wind, merid_wind):
    eastward = jnp.roll(centre, -1, axis=-1)
    westward = jnp.roll(centre, 1, axis=-1)
    return (
        -(zonal_wind + centre) * (eastward - westward) * 0.5
        - merid_wind * (above_row - below_row) * 0.5
    )


def band_mask(bounds, first_row, row_total):
    row_ids = first_row + lax.broadcasted_iota(jnp.int32, (1, row_total, 1), 1)
    lower_edge = bounds[:, 0][:, None, None]
    upper_edge = bounds[:, 1][:, None, None]
    return ((row_ids >= lower_edge) & (row_ids < upper_edge)).astype(jnp.float32)


def folded_matrix(lon_count):
    half = lon_count // 2
    waves = np.arange(M).reshape(M // 2, 2).T.reshape(2, 1, M // 2, 1)
    turns = (waves * np.arange(half)) % lon_count
    angles = turns * (2.0 * math.pi / lon_count)
    both = np.concatenate([np.cos(angles), -np.sin(angles)], axis=1) / math.sqrt(lon_count)
    both = both.reshape(2, 2, 2, M // 4, half).transpose(0, 2, 1, 3, 4)
    return both.reshape(2 * M, half).astype(ml_dtypes.bfloat16)


def schedule(slots, cols):
    chunks = slots // GROUP
    phases = [0]
    for tile in range(cols // TILE):
        share = min(1.0, (tile + 1) * TILE / cols)
        needed = share * slots + 3.5 * math.sqrt(slots * share * (1.0 - share) / 3.0) + 1.0
        phase = min(chunks - 1, math.ceil(needed / GROUP) - 1)
        phases.append(max(phases[-1], phase))
    phases = phases[1:]
    return [phases[tile // 2 * 2 + 1] for tile in range(len(phases))] + [chunks - 1]


def flipped(value, bits, size):
    result, bit = 0, 1
    while bit < size:
        digit = (value // bit) % 2
        result = result + bit * ((1 - digit) if bits & bit else digit)
        bit *= 2
    return result


def fused_kernel(
    dims,
    band,
    waves,
    field,
    zonal,
    merid,
    matrix_source,
    legendre,
    total,
    kept,
    table_out,
    table,
    numbers,
    entries,
    x,
    section,
    wind_zonal,
    wind_merid,
    edge,
    halo_out,
    halo_in,
    folded,
    matrix,
    natural_first,
    natural,
    pick,
    outgoing_first,
    received_first,
    outgoing,
    received,
    stage,
    ordered,
    ring_main,
    ring_rest,
    tail_main,
    tail_rest,
    edge_sem,
    field_sem,
    matrix_sem,
    halo_send,
    halo_recv,
    send_sem,
    recv_sem,
    own_sem,
    send_first,
    recv_first,
    own_first,
    ring_sem,
    tail_sem,
    kept_sem,
    table_sem,
):
    lat_size, fld_size, rep_size = dims
    lat, fld, rep = lax.axis_index("lat"), lax.axis_index("fld"), lax.axis_index("rep")
    levels, rows, length = field.shape
    parts = length // LANES
    half = parts // 2
    groups = lat_size * fld_size
    chunks, origins = received.shape[0], received.shape[1]
    slots = chunks * GROUP
    bands = lat_size * rep_size
    rest = rows - LANES
    width = folded.shape[1]
    position = lat * rep_size + rep
    peers = bands
    waves_half = M // 2
    cols = legendre.shape[2]
    tiles = cols // TILE
    steps = cols // WIDE
    tail = cols - tiles * TILE
    start = position * rows

    edge_copies = []
    for side, first in enumerate((0, rows - 8)):
        for array, source in enumerate((field, zonal, merid)):
            edge_copies.append(
                pltpu.make_async_copy(
                    source.at[:, first : first + 8, :], edge.at[side, array], edge_sem.at[side, array]
                )
            )
    for copy in edge_copies:
        copy.start()

    def column_copy(level, part):
        return pltpu.make_async_copy(
            field.at[level, :, part * LANES : (part + 1) * LANES],
            x.at[level, part, PAD : PAD + rows, :],
            field_sem.at[level, part],
        )

    def wind_copies(level):
        return (
            pltpu.make_async_copy(
                zonal.at[level], wind_zonal.at[level, 8 : 8 + rows, :], field_sem.at[level, parts]
            ),
            pltpu.make_async_copy(
                merid.at[level], wind_merid.at[level, 8 : 8 + rows, :], field_sem.at[level, parts + 1]
            ),
        )

    @pl.loop(0, levels)
    def _(level):
        for part in range(parts):
            column_copy(level, part).start()

        for copy in wind_copies(level):
            copy.start()

    barrier = pltpu.get_barrier_semaphore()
    everyone = lat_size * fld_size * rep_size
    lats = [flipped(lat, bits, lat_size) for bits in range(lat_size)]
    flds = [flipped(fld, bits, fld_size) for bits in range(fld_size)]
    reps = [flipped(rep, bits, rep_size) for bits in range(rep_size)]
    for i in range(lat_size):
        for j in range(fld_size):
            for k in range(rep_size):
                if i + j + k > 0:
                    pl.semaphore_signal(
                        barrier, inc=1, device_id=(lats[i], flds[j], reps[k]), device_id_type=MESH
                    )

    block_rows = waves_half // 2

    matrix_copy = pltpu.make_async_copy(matrix_source, matrix, matrix_sem)
    matrix_copy.start()
    above = lax.rem(position + peers - 1, peers)
    below = lax.rem(position + 1, peers)

    def halo_copy(side):
        target = (above, below)[side]
        return pltpu.make_async_remote_copy(
            src_ref=halo_out.at[side],
            dst_ref=halo_in.at[1 - side],
            send_sem=halo_send.at[side],
            recv_sem=halo_recv.at[1 - side],
            device_id=(target // rep_size, fld, target % rep_size),
            device_id_type=MESH,
        )

    filled = levels * rows
    folded[:, filled:width, :] = jnp.zeros((2, width - filled, folded.shape[2]), jnp.bfloat16)


    chosen = waves[...]
    chosen = jnp.where(
        chosen >= 0, lax.shift_right_arithmetic(chosen, 1) + (chosen & 1) * waves_half, -1
    )
    numbers[...] = chosen.T
    exists = (position > 0, position < peers - 1)
    for copy in edge_copies:
        copy.wait()
    for part in range(parts):
        lanes = slice(part * LANES, (part + 1) * LANES)
        for level in range(levels):
            for side, (pair, single) in enumerate((((0, 2), (0, 1)), ((6, 8), (7, 8)))):
                halo_out[side, part, 2 * level : 2 * level + 2, :] = edge[
                    side, 0, level, pair[0] : pair[1], lanes
                ]
                for array in (1, 2):
                    row = (array + 1) * levels + level
                    halo_out[side, part, row : row + 1, :] = edge[
                        side, array, level, single[0] : single[1], lanes
                    ]
    def slopes(centre_of, next_of, previous_of, zonal_of, merid_of, scale, last_lane, first_lane):
        centres, easts, wests = {}, {}, {}

        def turn(part):
            if part not in centres:
                centres[part] = centre_of(part)
                easts[part] = pltpu.roll(centres[part], LANES - 1, axis=1)
                wests[part] = pltpu.roll(centres[part], 1, axis=1)

        def slope(part):
            after, before = (part + 1) % parts, (part - 1) % parts
            for needed in (part, after, before):
                turn(needed)
            east = jnp.where(last_lane, easts[after], easts[part])
            west = jnp.where(first_lane, wests[before], wests[part])
            centre = centres[part]
            return centre, scale * (
                (zonal_of(part) + centre) * (west - east)
                + merid_of(part) * (previous_of(part) - next_of(part))
            )

        return slope

    def scale_of(level, first_row, count):
        lower, upper = band[0, fld * levels + level], band[1, fld * levels + level]
        ids = start + first_row + lax.broadcasted_iota(jnp.int32, (count, LANES), 0)
        return jnp.where((ids >= lower) & (ids < upper), 0.5, 0.0)

    def edges_of(count):
        lane = lax.broadcasted_iota(jnp.int32, (count, LANES), 1)
        return lane == LANES - 1, lane == 0

    def greet():
        pl.semaphore_wait(barrier, everyone - 1)
        for side in range(2):

            @pl.when(exists[side])
            def _():
                halo_copy(side).start()

            @pl.when(jnp.logical_not(exists[side]))
            def _():
                halo_in[side] = jnp.zeros(halo_in.shape[1:], jnp.float32)

    def first_section(level, block):
        first = pl.multiple_of(block * 8, 8)
        at = pl.multiple_of(first + PAD - 8, 8)
        slope = slopes(
            lambda part: x[level, part, pl.ds(at, 8), :],
            lambda part: x[level, part, pl.ds(at + 1, 8), :],
            lambda part: x[level, part, pl.ds(at - 1, 8), :],
            lambda part: wind_zonal[level, pl.ds(first, 8), part * LANES : (part + 1) * LANES],
            lambda part: wind_merid[level, pl.ds(first, 8), part * LANES : (part + 1) * LANES],
            scale_of(level, first - 8, 8),
            *edges_of(8),
        )
        for part in range(parts):
            centre, change = slope(part)
            section[level, part, pl.ds(at, 8), :] = centre + change

    @pl.loop(0, levels)
    def _(level):
        for part in range(parts):
            column_copy(level, part).wait()

        for copy in wind_copies(level):
            copy.wait()

        @pl.loop(2, rows // 8)
        def _(block):
            first_section(level, block)

        @pl.when(level == 0)
        def _():
            greet()

    for side in range(2):

        @pl.when(exists[side])
        def _():
            halo_copy(1 - side).wait_recv()

    for part in range(parts):
        lanes = slice(part * LANES, (part + 1) * LANES)
        for level in range(levels):
            pair = slice(2 * level, 2 * level + 2)
            x[level, part, PAD - 2 : PAD, :] = halo_in[0, part, pair, :]
            x[level, part, PAD + rows : PAD + rows + 2, :] = halo_in[1, part, pair, :]
            for array, wind in ((1, wind_zonal), (2, wind_merid)):
                row = (array + 1) * levels + level
                wind[level, 7:8, lanes] = halo_in[0, part, row : row + 1, :]
                wind[level, 8 + rows : 9 + rows, lanes] = halo_in[1, part, row : row + 1, :]

    def boundary_rows(level):
        @pl.loop(0, 4)
        def _(side):
            first_section(level, side % 2 + side // 2 * (rows // 8))

    def second_section(level):
        @pl.loop(0, rows // SUB)
        def _(block):
            first = pl.multiple_of(block * SUB, SUB)
            at = pl.multiple_of(first + PAD, SUB)
            wind_at = pl.multiple_of(first + 8, 8)
            slope = slopes(
                lambda part: section[level, part, pl.ds(at, SUB), :],
                lambda part: section[level, part, pl.ds(at + 1, SUB), :],
                lambda part: section[level, part, pl.ds(at - 1, SUB), :],
                lambda part: wind_zonal[level, pl.ds(wind_at, SUB), part * LANES : (part + 1) * LANES],
                lambda part: wind_merid[level, pl.ds(wind_at, SUB), part * LANES : (part + 1) * LANES],
                scale_of(level, first, SUB),
                *edges_of(SUB),
            )

            def advected(part):
                centre, change = slope(part)
                return 0.5 * (x[level, part, pl.ds(at, SUB), :] + centre + change)

            late = first // LANES
            goes = (1 - late) * (level * LANES + first) + late * (
                levels * LANES + level * rest + first - LANES
            )
            goes = pl.ds(pl.multiple_of(goes, SUB), SUB)
            for part in range(half):
                near, far = advected(part), advected(part + half)
                lanes = slice(part * LANES, (part + 1) * LANES)
                folded[0, goes, lanes] = (near + far).astype(jnp.bfloat16)
                folded[1, goes, lanes] = (near - far).astype(jnp.bfloat16)

    boundary_rows(0)
    second_section(0)
    matrix_copy.wait()

    def product(block, values):
        here = pl.ds(pl.multiple_of(block * block_rows, SUB), block_rows)
        return lax.dot_general(
            matrix[here, :], values, (((1,), (1,)), ((), ())), preferred_element_type=jnp.float32
        ).astype(jnp.bfloat16)

    @pl.loop(0, 4)
    def _(quarter):
        for side in range(2):
            there = pl.ds(pl.multiple_of(quarter * block_rows, SUB), block_rows)
            natural_first[there, side * LANES : (side + 1) * LANES] = product(
                2 * quarter + side, folded[quarter // 2, 0:LANES, :]
            )

    half_flds = fld_size // rep_size
    to_rep = fld // half_flds
    place = ((fld % half_flds) * lat_size + lat) * rep_size + rep
    own = lat * fld_size + fld
    stays = to_rep == rep
    hops = [(i, j) for i in range(lat_size - 1, -1, -1) for j in range(fld_size - 1, -1, -1)]

    def sending(chunk, index):
        far_lat = flipped(lat, hops[index][0], lat_size)
        far_fld = flipped(fld, hops[index][1], fld_size)
        return pltpu.make_async_remote_copy(
            src_ref=outgoing.at[chunk, far_lat * fld_size + far_fld],
            dst_ref=received.at[chunk, place],
            send_sem=send_sem.at[chunk, index],
            recv_sem=recv_sem.at[chunk, place],
            device_id=(far_lat, far_fld, to_rep),
            device_id_type=MESH,
        )

    def keeping(chunk):
        return pltpu.make_async_copy(
            outgoing.at[chunk, own], received.at[chunk, place], own_sem.at[chunk]
        )

    pairs = SUB // GROUP

    def picked_rows(several):
        near = numbers[pl.ds(pl.multiple_of(several * SUB, SUB), SUB), :]
        lane = lax.broadcasted_iota(jnp.int32, (GROUP, M), 1)
        for piece in range(pairs):
            for group in range(groups):
                at = (piece * groups + group) * GROUP
                column = near[piece * GROUP : (piece + 1) * GROUP, group : group + 1]
                pick[at : at + GROUP, :] = jnp.where(column == lane, 1.0, 0.0)
        return pick[...].astype(jnp.bfloat16)

    def send_pair(several):
        picked = picked_rows(several)
        sides = [
            jnp.dot(picked, natural[side], preferred_element_type=jnp.float32) for side in range(2)
        ]
        for piece in range(pairs):
            chunk = several * pairs + piece
            for group in range(groups):
                at = (piece * groups + group) * GROUP
                outgoing[chunk, group] = jnp.concatenate(
                    [side[at : at + GROUP, :] for side in sides], axis=0
                ).astype(jnp.bfloat16)
            for index in range(groups - 1):
                sending(chunk, index).start()

            @pl.when(stays)
            def _():
                keeping(chunk).start()

            @pl.when(jnp.logical_not(stays))
            def _():
                sending(chunk, groups - 1).start()

    def sending_first(index):
        far_lat = flipped(lat, hops[index][0], lat_size)
        far_fld = flipped(fld, hops[index][1], fld_size)
        return pltpu.make_async_remote_copy(
            src_ref=outgoing_first.at[far_lat * fld_size + far_fld],
            dst_ref=received_first.at[place],
            send_sem=send_first.at[index],
            recv_sem=recv_first.at[place],
            device_id=(far_lat, far_fld, to_rep),
            device_id_type=MESH,
        )

    keeping_first = pltpu.make_async_copy(
        outgoing_first.at[own], received_first.at[place], own_first
    )

    @pl.loop(0, chunks // pairs)
    def _(several):
        both = jnp.dot(picked_rows(several), natural_first[...], preferred_element_type=jnp.float32)
        for piece in range(pairs):
            for group in range(groups):
                at = (piece * groups + group) * GROUP
                outgoing_first[group, several * pairs + piece] = jnp.concatenate(
                    [both[at : at + GROUP, 0:LANES], both[at : at + GROUP, LANES : 2 * LANES]], axis=0
                ).astype(jnp.bfloat16)

    for index in range(groups - 1):
        sending_first(index).start()

    @pl.when(stays)
    def _():
        keeping_first.start()

    @pl.when(jnp.logical_not(stays))
    def _():
        sending_first(groups - 1).start()

    def ring_copies(tile, slot):
        columns = pl.ds(pl.multiple_of(tile * WIDE, WIDE), WIDE)
        return (
            pltpu.make_async_copy(
                legendre.at[:, 0:LANES, columns], ring_main.at[slot], ring_sem.at[slot, 0]
            ),
            pltpu.make_async_copy(
                legendre.at[:, LANES:rows, columns], ring_rest.at[slot], ring_sem.at[slot, 1]
            ),
        )

    for tile in range(min(RING, steps)):
        for copy in ring_copies(tile, tile):
            copy.start()
    tail_columns = slice(tiles * TILE, cols)
    tail_copies = (
        pltpu.make_async_copy(legendre.at[:, 0:LANES, tail_columns], tail_main, tail_sem.at[0]),
        pltpu.make_async_copy(legendre.at[:, LANES:rows, tail_columns], tail_rest, tail_sem.at[1]),
    )
    for copy in tail_copies:
        copy.start()


    stage[...] = jnp.zeros(stage.shape, jnp.float32)
    mine = waves[pl.ds(lat * fld_size + fld, 1), :]
    counts = jnp.where(mine >= 0, M - mine, 0)
    slot_row = lax.broadcasted_iota(jnp.int32, (LANES, slots), 0)
    slot_lane = lax.broadcasted_iota(jnp.int32, (LANES, slots), 1)
    begins = jnp.sum(jnp.where(slot_lane < slot_row, counts, 0), axis=1, keepdims=True)
    ends = jnp.sum(jnp.where(slot_lane <= slot_row, counts, 0), axis=1, keepdims=True)
    real = lax.broadcasted_iota(jnp.int32, (LANES, LANES), 0) < slots
    lane = lax.broadcasted_iota(jnp.int32, (LANES, LANES), 1)
    row = lax.broadcasted_iota(jnp.int32, (LANES, LANES), 0)
    starts_row = jnp.sum(jnp.where(row == lane, begins, 0), axis=0, keepdims=True)
    first = jnp.sum(jnp.where(real & (ends <= lane * TILE), 1, 0), axis=0, keepdims=True)
    limit = jnp.minimum(lane * TILE + TILE, cols)
    begun = jnp.sum(jnp.where(real & (begins < limit), 1, 0), axis=0, keepdims=True)
    tile_lane = lane[0:1, :]
    phases = schedule(slots, cols)
    bounds = [sum(phase < chunk for phase in phases[:tiles]) for chunk in range(chunks)] + [tiles]
    ready = jnp.full((1, LANES), GROUP, jnp.int32)
    for chunk in range(1, chunks):
        ready += jnp.where(tile_lane >= bounds[chunk], GROUP, 0)
    ready = jnp.where(tile_lane >= tiles, slots, ready)
    base_row = jnp.minimum(first, ready - WINDOW)
    extra = lax.shift_right_arithmetic(jnp.maximum(begun - base_row - 1, 0), WINDOW.bit_length() - 1)
    extra = jnp.where(tile_lane <= tiles, extra, 0)
    left = jnp.broadcast_to(jnp.sum(extra, axis=1, keepdims=True), (1, LANES))
    entries[...] = jnp.concatenate(
        [base_row, starts_row, extra, left, jnp.zeros((4, LANES), jnp.int32)], axis=0
    )
    table_copies = (
        pltpu.make_async_copy(entries, table, table_sem.at[0]),
        pltpu.make_async_copy(entries, table_out, table_sem.at[1]),
    )
    for copy in table_copies:
        copy.start()

    @pl.loop(1, levels)
    def _(level):
        boundary_rows(level)
        second_section(level)

    @pl.loop(0, 4)
    def _(quarter):
        for side in range(2):
            there = pl.ds(pl.multiple_of(quarter * block_rows, SUB), block_rows)
            natural[side, there, :] = product(
                2 * quarter + side, folded[quarter // 2, LANES:width, :]
            )

    def multiply(lhs, main_part, rest_part):
        depth = bands * LANES
        columns = main_part.shape[2]
        return jnp.dot(
            lhs[:, :depth], main_part.reshape(depth, columns), preferred_element_type=jnp.float32
        ) + jnp.dot(
            lhs[:, depth:], rest_part.reshape(bands * rest, columns), preferred_element_type=jnp.float32
        )

    def sums(tile, main_part, rest_part):
        window = table[0, tile]
        lhs = jnp.concatenate([ordered[window + slot] for slot in range(WINDOW)], axis=0)
        products = multiply(lhs, main_part, rest_part)
        columns = main_part.shape[2]
        ids = tile * TILE + lax.broadcasted_iota(jnp.int32, (SUB, columns), 1)
        held = jnp.zeros((SUB, columns), jnp.float32)
        for slot in range(WINDOW):
            held = jnp.where(
                ids >= table[1, window + slot], products[slot * SUB : (slot + 1) * SUB, :], held
            )
        return jnp.where(ids >= table[1, window + WINDOW], 0.0, held)

    for copy in table_copies:
        copy.wait()
    waiting = []
    for several in range(min(AHEAD, chunks // pairs)):
        send_pair(several)
    for origin in range(origins):

        @pl.when(jnp.logical_not(stays & (place == origin)))
        def _():
            pltpu.make_async_remote_copy(
                src_ref=received_first.at[origin],
                dst_ref=received_first.at[origin],
                send_sem=send_first.at[0],
                recv_sem=recv_first.at[origin],
                device_id=(lat, fld, 1 - rep),
                device_id_type=MESH,
            ).wait_recv()

    @pl.when(stays)
    def _():
        keeping_first.wait()

    for chunk in range(chunks):
        for origin in range(origins):

            @pl.when(jnp.logical_not(stays & (place == origin)))
            def _():
                pltpu.make_async_remote_copy(
                    src_ref=received.at[chunk, origin],
                    dst_ref=received.at[chunk, origin],
                    send_sem=send_sem.at[chunk, 0],
                    recv_sem=recv_sem.at[chunk, origin],
                    device_id=(lat, fld, 1 - rep),
                    device_id_type=MESH,
                ).wait_recv()

        @pl.when(stays)
        def _():
            keeping(chunk).wait()

        if chunk % pairs == 0 and chunk // pairs + AHEAD < chunks // pairs:
            send_pair(chunk // pairs + AHEAD)
        quads = LANES // rest

        @pl.loop(0, bands // quads)
        def _(quad):
            for part in range(origins // bands):
                for level in range(levels):
                    for side in range(2):
                        row = (part * levels + level) * 2 + side
                        spread = pl.ds(row, GROUP, stride=SUB)
                        from_rows = slice(side * GROUP, (side + 1) * GROUP)
                        pieces = []
                        for near in range(quads):
                            origin = part * bands + quad * quads + near
                            if level == 0:
                                whole = received_first[origin, chunk]
                            else:
                                whole = received[chunk, origin, :, (level - 1) * LANES : level * LANES]
                            stage[quad * quads + near, spread, :] = whole.astype(jnp.float32)[from_rows]
                            begin = (levels - 1) * LANES + level * rest
                            pieces.append(
                                received[chunk, origin, :, begin : begin + rest].astype(jnp.float32)[
                                    from_rows
                                ]
                            )
                        stage[bands + quad, spread, :] = jnp.concatenate(pieces, axis=1)

        slots_here = slice(chunk * GROUP, (chunk + 1) * GROUP)
        for part in range(stage.shape[0]):
            ordered[slots_here, :, part * LANES : (part + 1) * LANES] = (
                stage[part].astype(jnp.bfloat16).reshape(GROUP, SUB, LANES)
            )
        copy = pltpu.make_async_copy(ordered.at[slots_here], kept.at[slots_here], kept_sem.at[chunk])
        copy.start()
        waiting.append(copy)

        @pl.loop(bounds[chunk] // 2, bounds[chunk + 1] // 2)
        def _(tile):
            slot = lax.rem(tile, RING)
            for copy in ring_copies(tile, slot):
                copy.wait()
            for side in range(2):
                columns = slice(side * TILE, (side + 1) * TILE)
                held = sums(
                    2 * tile + side, ring_main[slot, :, :, columns], ring_rest[slot, :, :, columns]
                )
                here = pl.ds(pl.multiple_of(tile * WIDE + side * TILE, TILE), TILE)
                for level in range(total.shape[0]):
                    total[level, :, here] = held[2 * level : 2 * level + 2, :]
            following = tile + RING

            @pl.when(following < steps)
            def _():
                for copy in ring_copies(following, slot):
                    copy.start()

        if chunk == chunks - 1:
            for copy in tail_copies:
                copy.wait()
            held = sums(tiles, tail_main[...], tail_rest[...])
            for level in range(total.shape[0]):
                total[level, :, tiles * TILE : cols] = held[2 * level : 2 * level + 2, :]

    for side in range(2):

        @pl.when(exists[side])
        def _():
            halo_copy(side).wait_send()

    for index in range(groups - 1):
        sending_first(index).wait_send()

    @pl.when(jnp.logical_not(stays))
    def _():
        sending_first(groups - 1).wait_send()

    @pl.loop(0, chunks)
    def _(chunk):
        for index in range(groups - 1):
            sending(chunk, index).wait_send()

        @pl.when(jnp.logical_not(stays))
        def _():
            sending(chunk, groups - 1).wait_send()

    for copy in waiting:
        copy.wait()


def fused(dims, band, waves, field, wind_zonal, wind_merid, legendre):
    lat_size, fld_size, rep_size = dims
    levels, rows, length = field.shape
    groups = lat_size * fld_size
    slots = waves.shape[1]
    chunks = slots // GROUP
    bands = lat_size * rep_size
    origins = fld_size // rep_size * bands
    rest = rows - LANES
    parts = length // LANES
    width = pl.cdiv(levels * rows, LANES) * LANES
    depth = bands * rows
    cols = legendre.shape[2]
    tail = cols % TILE
    out_levels = origins // bands * levels
    matrix = jnp.asarray(folded_matrix(length))
    dma = pltpu.SemaphoreType.DMA
    smem = pl.BlockSpec(memory_space=pltpu.SMEM)
    vmem = pl.BlockSpec(memory_space=pltpu.VMEM)
    anywhere = pl.BlockSpec(memory_space=pltpu.HBM)
    return pl.pallas_call(
        functools.partial(fused_kernel, dims),
        out_shape=(
            jax.ShapeDtypeStruct((out_levels, 2, cols), jnp.float32),
            jax.ShapeDtypeStruct((slots, SUB, depth), jnp.bfloat16),
            jax.ShapeDtypeStruct((8, LANES), jnp.int32),
        ),
        in_specs=[smem, vmem] + [anywhere] * 5,
        out_specs=(vmem, anywhere, anywhere),
        scratch_shapes=[
            pltpu.SMEM((8, LANES), jnp.int32),
            pltpu.VMEM((slots, groups), jnp.int32),
            pltpu.VMEM((8, LANES), jnp.int32),
            pltpu.VMEM((levels, parts, rows + 2 * PAD, LANES), jnp.float32),
            pltpu.VMEM((levels, parts, rows + 2 * PAD, LANES), jnp.float32),
            pltpu.VMEM((levels, rows + 16, length), jnp.float32),
            pltpu.VMEM((levels, rows + 16, length), jnp.float32),
            pltpu.VMEM((2, 3, levels, 8, length), jnp.float32),
            pltpu.VMEM((2, parts, SUB, LANES), jnp.float32),
            pltpu.VMEM((2, parts, SUB, LANES), jnp.float32),
            pltpu.VMEM((2, width, length // 2), jnp.bfloat16),
            pltpu.VMEM((2 * M, length // 2), jnp.bfloat16),
            pltpu.VMEM((M, 2 * LANES), jnp.bfloat16),
            pltpu.VMEM((2, M, width - LANES), jnp.bfloat16),
            pltpu.VMEM((groups * SUB, M), jnp.float32),
            pltpu.VMEM((groups, chunks, 2 * GROUP, LANES), jnp.bfloat16),
            pltpu.VMEM((origins, chunks, 2 * GROUP, LANES), jnp.bfloat16),
            pltpu.VMEM((chunks, groups, 2 * GROUP, width - LANES), jnp.bfloat16),
            pltpu.VMEM((chunks, origins, 2 * GROUP, width - LANES), jnp.bfloat16),
            pltpu.VMEM((depth // LANES, GROUP * SUB, LANES), jnp.float32),
            pltpu.VMEM((slots, SUB, depth), jnp.bfloat16),
            pltpu.VMEM((RING, bands, LANES, WIDE), jnp.bfloat16),
            pltpu.VMEM((RING, bands, rest, WIDE), jnp.bfloat16),
            pltpu.VMEM((bands, LANES, tail), jnp.bfloat16),
            pltpu.VMEM((bands, rest, tail), jnp.bfloat16),
            dma((2, 3)),
            dma((levels, parts + 2)),
            dma,
            dma((2,)),
            dma((2,)),
            dma((chunks, groups)),
            dma((chunks, origins)),
            dma((chunks,)),
            dma((groups,)),
            dma((origins,)),
            dma,
            dma((RING, 2)),
            dma((2,)),
            dma((chunks,)),
            dma((2,)),
        ],
        compiler_params=pltpu.CompilerParams(
            collective_id=0, has_side_effects=True, vmem_limit_bytes=LIMIT
        ),
    )(band, waves, field, wind_zonal, wind_merid, matrix, legendre)


def finish_kernel(
    rest, table, partial, kept, legendre, out, window_rows, main, tail, held, sem, out_sem
):
    slots = kept.shape[0]
    bands = legendre.shape[0]
    cols = legendre.shape[2]
    depth = bands * LANES

    def moved(source, target):
        copy = pltpu.make_async_copy(source, target, sem)
        copy.start()
        copy.wait()

    copies = [
        pltpu.make_async_copy(partial.at[level], out.at[level], out_sem.at[level])
        for level in range(partial.shape[0])
    ]
    for copy in copies:
        copy.start()
    for copy in copies:
        copy.wait()

    @pl.when(table[3, 0] > 0)
    def _():
        @pl.loop(0, pl.cdiv(cols, TILE))
        def _(tile):
            @pl.loop(0, table[2, tile])
            def _(turn):
                begin = table[0, tile] + WINDOW * (turn + 1)
                window = jnp.minimum(begin, slots - WINDOW)
                moved(kept.at[pl.ds(window, WINDOW)], window_rows)
                lhs = window_rows[...].reshape(WINDOW * SUB, kept.shape[2])

                @pl.loop(0, jnp.minimum(TILE, cols - tile * TILE) // LANES)
                def _(piece):
                    first = pl.multiple_of(tile * TILE + piece * LANES, LANES)
                    here = pl.ds(first, LANES)
                    moved(legendre.at[:, 0:LANES, here], main)
                    moved(legendre.at[:, LANES : LANES + rest, here], tail)
                    moved(out.at[:, :, here], held)
                    products = jnp.dot(
                        lhs[:, :depth], main[...].reshape(depth, LANES), preferred_element_type=jnp.float32
                    ) + jnp.dot(
                        lhs[:, depth:],
                        tail[...].reshape(bands * rest, LANES),
                        preferred_element_type=jnp.float32,
                    )
                    ids = first + lax.broadcasted_iota(jnp.int32, (SUB, LANES), 1)
                    more = jnp.zeros((SUB, LANES), jnp.float32)
                    for slot in range(WINDOW):
                        more = jnp.where(
                            ids >= table[1, window + slot], products[slot * SUB : (slot + 1) * SUB, :], more
                        )
                    more = jnp.where(
                        (ids >= table[1, begin]) & (ids < table[1, window + WINDOW]), more, 0.0
                    )
                    for level in range(held.shape[0]):
                        held[level] += more[2 * level : 2 * level + 2, :]
                    moved(held, out.at[:, :, here])


def finish(table, partial, kept, legendre):
    bands, rows, _ = legendre.shape
    smem = pl.BlockSpec(memory_space=pltpu.SMEM)
    vmem = pl.BlockSpec(memory_space=pltpu.VMEM)
    anywhere = pl.BlockSpec(memory_space=pltpu.HBM)
    return pl.pallas_call(
        functools.partial(finish_kernel, rows - LANES),
        out_shape=jax.ShapeDtypeStruct(partial.shape, partial.dtype),
        in_specs=[smem, vmem, anywhere, anywhere],
        out_specs=anywhere,
        scratch_shapes=[
            pltpu.VMEM((WINDOW,) + kept.shape[1:], jnp.bfloat16),
            pltpu.VMEM((bands, LANES, LANES), jnp.bfloat16),
            pltpu.VMEM((bands, rows - LANES, LANES), jnp.bfloat16),
            pltpu.VMEM((partial.shape[0], 2, LANES), jnp.float32),
            pltpu.SemaphoreType.DMA,
            pltpu.SemaphoreType.DMA((partial.shape[0],)),
        ],
        compiler_params=pltpu.CompilerParams(vmem_limit_bytes=LIMIT),
    )(table, partial, kept, legendre)


def body(field, wind_zonal, wind_merid, band, waves, legendre):
    field_count, row_count, lon_count = field.shape
    lat_size = lax.axis_size("lat")
    fld_size = lax.axis_size("fld")
    rep_size = lax.axis_size("rep")
    first_row = (lax.axis_index("lat") * rep_size + lax.axis_index("rep")) * row_count
    slot_count = waves.shape[1]
    rest = row_count - LANES
    direct = (
        rest > 0
        and rest % SUB == 0
        and LANES % rest == 0
        and lat_size * rep_size % (LANES // rest) == 0
        and field_count * 4 <= SUB
        and slot_count % SUB == 0
        and slot_count + WINDOW < LANES
        and legendre.shape[2] // TILE < LANES
        and lon_count == 2 * M
        and lon_count % (2 * LANES) == 0
        and legendre.shape[2] % LANES == 0
        and legendre.shape[2] > WIDE
        and 0 < legendre.shape[2] % WIDE < TILE
        and rep_size == 2
        and fld_size % 2 == 0
        and fld_size // rep_size * field_count * 2 <= SUB
        and lat_size & (lat_size - 1) == 0
        and fld_size & (fld_size - 1) == 0
        and lat_size * fld_size <= 16
    )
    if direct:
        columns = legendre.reshape(lat_size * rep_size, row_count, legendre.shape[2])
        partial, kept, table = fused(
            (lat_size, fld_size, rep_size),
            band.T, waves, field, wind_zonal, wind_merid, columns,
        )
        return finish(table, partial, kept, columns)[None]
    bounds = lax.dynamic_slice_in_dim(band, lax.axis_index("fld") * field_count, field_count, 0)
    in_band = band_mask(bounds, first_row, row_count)
    padded = with_halo(field, ((("lat", "rep"), 1),), 1)
    first_section = field + in_band * tendency(
        field, padded[:, 2:], padded[:, :-2], wind_zonal, wind_merid
    )
    padded_section = with_halo(first_section, ((("lat", "rep"), 1),), 1)
    advected = 0.5 * (
        field
        + first_section
        + in_band
        * tendency(
            first_section, padded_section[:, 2:], padded_section[:, :-2], wind_zonal, wind_merid
        )
    )
    grid_low = advected.astype(jnp.bfloat16)
    spectra = jnp.dot(
        grid_low.reshape(field_count * row_count, lon_count),
        dft_matrix(lon_count, M),
        preferred_element_type=jnp.float32,
    ).astype(jnp.bfloat16)
    spectra = spectra.reshape(field_count, row_count, 2, M)
    wave_index = jnp.where(waves >= 0, waves, 0)
    picked = jnp.take(spectra, wave_index.reshape(-1), axis=3)
    picked = picked.reshape(field_count, row_count, 2, lat_size, fld_size, slot_count)
    outgoing = jnp.transpose(picked, (5, 2, 4, 0, 3, 1)).reshape(
        slot_count, 2, fld_size * field_count, lat_size * row_count
    )
    received = lax.all_to_all(
        lax.all_to_all(outgoing, "lat", split_axis=3, concat_axis=3, tiled=True),
        "fld",
        split_axis=2,
        concat_axis=2,
        tiled=True,
    )
    group = lax.axis_index("lat") * fld_size + lax.axis_index("fld")
    own_waves = lax.dynamic_index_in_dim(waves, group, 0, keepdims=False)
    counts = jnp.where(own_waves >= 0, M - own_waves, 0)
    offsets = jnp.cumsum(counts) - counts
    col_count = legendre.shape[2]
    col_ids = lax.broadcasted_iota(jnp.int32, (slot_count, col_count), 1)
    segments = ((col_ids >= offsets[:, None]) & (col_ids < (offsets + counts)[:, None])).astype(
        jnp.float32
    )
    total_fields = fld_size * field_count
    regrouped = lax.all_to_all(received, "rep", split_axis=2, concat_axis=3, tiled=True)
    half_fields = total_fields // rep_size
    ordered = regrouped.reshape(slot_count, 2, half_fields, rep_size, lat_size, row_count)
    ordered = jnp.transpose(ordered, (0, 1, 2, 4, 3, 5)).reshape(
        slot_count * 2 * half_fields, rep_size * lat_size * row_count
    )
    products = jnp.dot(ordered, legendre[0], preferred_element_type=jnp.float32)
    spectrum = jnp.einsum(
        "scfk,sk->fck", products.reshape(slot_count, 2, half_fields, col_count), segments
    )
    return spectrum[None]


def solution(mesh):
    placed = (
        P("fld", ("lat", "rep"), None),
        P("fld", ("lat", "rep"), None),
        P("fld", ("lat", "rep"), None),
        P(),
        P(),
        P(("lat", "fld"), None, None),
    )
    return jax.shard_map(
        body,
        mesh=mesh,
        in_specs=placed,
        out_specs=P(("lat", "fld"), "rep", None, None),
        check_vma=False,
    )
```
